128 devices in a mesh: rows: 4 (over z), vocab: 32 (over x, y, core).
Axes of the slice: x: 4, y: 4, z: 4, core: 2. Of those that a mesh axis runs over, the one named last changes fastest.
Arguments:
- expert_delta: bfloat16 [512, 32000], P(None, ('rows', 'vocab')), may hold values from -24 to 24
- small_anchors: bfloat16 [32000, 2048], P(('rows', 'vocab')), may hold values from -0.18 to 0.18
- small_tokens: int32 [2048], replicated, may hold values from 0 to 31999, as said below
- base_logits: float32 [512, 128256], P('rows', 'vocab'), may hold values from -2 to 300
- base_anchors: bfloat16 [128256, 2048], P('vocab'), may hold values from -0.18 to 0.18
- base_tokens: int32 [2048], replicated, may hold values from 0 to 128255, as said below
- active_rows: int32 [512], P('rows'), may hold values 0 or 1
Outputs:
- logit_update: float32 [512, 128256], P('rows', 'vocab')
The draws below stay inside these ranges and needn't reach their ends.
Inputs may be any that keep to these rules, and one draw needn't show every extreme that they name: `small_tokens`: 2048 distinct token ids, the first and last ids of the small vocabulary among them. `base_tokens`: 2048 distinct token ids, the first and last ids of the base vocabulary among them.
All inputs are finite; a program needn't handle non-finite values. No bound on the sum of `active_rows` on one device may be relied on, other than what follows from the above.
Results may differ from the reference program's by a relative error of at most 0.03.
Values may be sent and summed in bfloat16 or wider, within the bound.
No kernel may reach another device: no remote copies, remote signals or barrier semaphores. Data moves between devices by JAX's collectives and lax.ppermute only.
A program may use at most 128 MiB of HBM per device.

```python
import math
import jax
import jax.numpy as jnp
from jax import lax

BASE_VOCAB = 128256
SMALL_VOCAB = 32000
ANCHORS = 2048
ITERATIONS = 3
ALL_ROWS = 512


def anchor_table(key, row_count):
    value_key, scale_key = jax.random.split(key)
    column_scale = jnp.exp(jax.random.uniform(scale_key, (ANCHORS,), minval=math.log(0.4), maxval=math.log(4.0)))
    noise = jnp.clip(jax.random.normal(value_key, (row_count, ANCHORS)), -4.0, 4.0)
    return (noise * column_scale[None, :] * 0.011).astype(jnp.bfloat16)


def token_choice(key, vocab_size):
    pick_key, order_key = jax.random.split(key)
    middle = jax.random.permutation(pick_key, vocab_size - 2)[:ANCHORS - 2] + 1
    joined = jnp.concatenate([jnp.zeros((1,), jnp.int32), middle.astype(jnp.int32), jnp.full((1,), vocab_size - 1, jnp.int32)])
    return jax.random.permutation(order_key, joined).astype(jnp.int32)


def draw_small_anchors(key, part):
    return anchor_table(jax.random.fold_in(key, 1), SMALL_VOCAB)


def draw_base_anchors(key, part):
    return anchor_table(jax.random.fold_in(key, 2), BASE_VOCAB)


def draw_small_tokens(key, part):
    return token_choice(jax.random.fold_in(key, 3), SMALL_VOCAB)


def draw_base_tokens(key, part):
    return token_choice(jax.random.fold_in(key, 4), BASE_VOCAB)


def draw_base_logits(key, part):
    value_key = jax.random.fold_in(jax.random.fold_in(key, 5), 0)
    rising = jnp.arange(BASE_VOCAB, dtype=jnp.float32) / BASE_VOCAB
    return 0.5 * jnp.clip(jax.random.normal(value_key, (ALL_ROWS, BASE_VOCAB)), -4.0, 4.0) + 1.1 * rising[None, :]


def touch_ends(result, stream_key, smallest, high):
    place = [jax.random.randint(jax.random.fold_in(stream_key, axis), (), 0, length) for axis, length in enumerate(result.shape)]
    main_axis = result.shape.index(max(result.shape))
    neighbour = place[:main_axis] + [(place[main_axis] + 1) % result.shape[main_axis]] + place[main_axis + 1:]
    return result.at[tuple(place)].set(smallest).at[tuple(neighbour)].set(high)


def spiked(result, stream_key, source, target, parts, factor):
    def block_of(axis_at):
        return (jnp.arange(result.shape[axis_at]) // (result.shape[axis_at] // parts)).reshape((-1,) + (1,) * (result.ndim - 1 - axis_at))

    near = jax.random.permutation(stream_key, parts)[block_of(target)]
    second = (block_of(target) + parts // 2) % parts
    return jnp.where((block_of(source) == near) | (block_of(source) == second), factor * result, result)


def block_scale(rng, shape, pieces, least, top_value):
    level = 1.0
    for position, parts in pieces:
        heights = jax.random.uniform(jax.random.fold_in(jax.random.fold_in(rng, 6), position), (parts,), jnp.float32, least / len(pieces), top_value / len(pieces))
        level = level * jnp.repeat(jnp.exp(heights), shape[position] // parts).reshape((-1,) + (1,) * (len(shape) - 1 - position))
    return level


def heavy_noise(rng, shape, width, reach, pieces, heavy, kind=jnp.bfloat16):
    values = width * jax.random.normal(rng, shape, jnp.float32)
    if pieces:
        values = values * block_scale(rng, shape, pieces, -0.22, 0.18)
    return jnp.clip(spiked(values, jax.random.fold_in(rng, 3), *heavy), -reach, reach).astype(kind)


def setup_inputs(seed: int = 0) -> dict:
    key_of = jax.random.split(jax.random.key(seed), 8)
    expert_delta = heavy_noise(key_of[0], (ALL_ROWS, SMALL_VOCAB), 1.0, 24.0, ((1, 128),), (1, 0, 128, 5.5))
    small_anchors = draw_small_anchors(jax.random.fold_in(key_of[7], 71), 0)
    small_tokens = draw_small_tokens(jax.random.fold_in(key_of[7], 71), 0)
    base_logits = draw_base_logits(jax.random.fold_in(key_of[7], 71), 0)
    base_anchors = draw_base_anchors(jax.random.fold_in(key_of[7], 71), 0)
    base_tokens = draw_base_tokens(jax.random.fold_in(key_of[7], 71), 0)
    active_rows = touch_ends((jax.random.randint(key_of[6], (ALL_ROWS,), 0, 4) < 3).astype(jnp.int32), jax.random.fold_in(key_of[6], 1), 0, 1)
    return dict(expert_delta=expert_delta, small_anchors=small_anchors, small_tokens=small_tokens, base_logits=base_logits, base_anchors=base_anchors, base_tokens=base_tokens, active_rows=active_rows)


epsilon = 1e-06
step_size = 2.0

def reference(expert_delta, small_anchors, small_tokens, base_logits, base_anchors, base_tokens, active_rows):
    target = jnp.dot(expert_delta, small_anchors, preferred_element_type=jnp.float32)
    target = target + expert_delta[:, small_tokens].astype(jnp.float32)
    mask = active_rows.astype(jnp.float32)[:, None]
    logits = base_logits
    logit_update = jnp.zeros_like(base_logits)
    for turn in range(ITERATIONS):
        row_max = lax.optimization_barrier(jnp.max(logits, axis=1, keepdims=True))
        weights = jnp.exp(logits - row_max)
        weights_low = weights.astype(jnp.bfloat16)
        total = lax.optimization_barrier(jnp.sum(weights, axis=1, keepdims=True))
        mass = jnp.dot(weights_low, base_anchors, preferred_element_type=jnp.float32)
        mass = mass + weights_low[:, base_tokens].astype(jnp.float32)
        related = BASE_VOCAB * mass / total
        gap = related - target
        direction = (gap * lax.rsqrt(lax.optimization_barrier(jnp.mean(gap * gap, axis=1, keepdims=True)) + epsilon)).astype(jnp.bfloat16)
        back = jnp.dot(direction, base_anchors.T, preferred_element_type=jnp.float32)
        back = back.at[:, base_tokens].add(direction.astype(jnp.float32))
        slope = lax.optimization_barrier(jnp.sum(weights * back, axis=1, keepdims=True)) / total
        change = -step_size * mask * weights * (back - slope)
        logits = logits + change
        logit_update = logit_update + change
    return logit_update
```

```python
import functools
import jax
import jax.numpy as jnp
from jax import lax
from jax.experimental import pallas as pl
from jax.experimental.pallas import tpu as pltpu
from jax.sharding import Mesh
from jax.sharding import PartitionSpec as P

ITERATIONS = 3
VOCAB = ("x", "y", "core")
CHIPS = ("rows", "x", "y")
LANES = 128
CHUNK = 512
epsilon = 1e-06
step_size = 2.0

HBM = pl.BlockSpec(memory_space=pl.ANY)
VMEM = pl.BlockSpec(memory_space=pltpu.VMEM)
SMEM = pl.BlockSpec(memory_space=pltpu.SMEM)


def chunks_of(extent):
    starts = list(range(0, extent, CHUNK))
    return [(start, min(CHUNK, extent - start)) for start in starts]


def three_parts(value):
    high = value.astype(jnp.bfloat16).astype(jnp.float32)
    rest = value - high
    middle = rest.astype(jnp.bfloat16).astype(jnp.float32)
    return high, middle, rest - middle


def matmul_nt(left, right):
    return lax.dot_general(left, right, (((1,), (1,)), ((), ())), preferred_element_type=jnp.float32)


def with_self(block, tokens, start):
    rows, columns = block.shape
    if rows % 16 == 0:
        place = lax.broadcasted_iota(jnp.int16, (rows, columns), 0) + jnp.int16(start)
        wanted = jnp.broadcast_to(tokens[None], (rows // 16, 16, columns)).reshape(rows, columns)
    else:
        place = lax.broadcasted_iota(jnp.int16, (rows, columns), 0) + jnp.int16(start)
        whole = -(-rows // 16)
        wanted = jnp.broadcast_to(tokens[None], (whole, 16, columns)).reshape(whole * 16, columns)[:rows]
    return jnp.where(place == wanted, block + jnp.bfloat16(1), block)


def put_masses(logits_ref, anchors_of, out_ref, mass_ref):
    extent, rows = logits_ref.shape
    top = jnp.max(logits_ref[...], axis=0, keepdims=True)
    total = jnp.zeros((1, rows), jnp.float32)
    for start, size in chunks_of(extent):
        weights = jnp.exp(logits_ref[pl.ds(start, size), :] - top)
        total = total + jnp.sum(weights, axis=0, keepdims=True)
        turned = weights.T.astype(jnp.bfloat16)
        part = jnp.dot(turned, anchors_of(start, size), preferred_element_type=jnp.float32)
        if start == 0:
            mass_ref[...] = part
        else:
            mass_ref[...] += part
    groups, halves, eight, width = out_ref.shape
    half = width - LANES
    for h in range(halves):
        piece = mass_ref[:, h * half : (h + 1) * half].reshape(groups, eight, half)
        out_ref[:, h, :, :half] = piece.astype(jnp.bfloat16)
    parts = three_parts(top) + three_parts(total)
    stats = jnp.concatenate(list(parts) + [jnp.zeros((LANES - len(parts), rows), jnp.float32)], axis=0)
    stats = stats.T.reshape(groups, eight, LANES).astype(jnp.bfloat16)
    for h in range(halves):
        out_ref[:, h, :, half:] = stats


def first_kernel(tokens_ref, anchors_ref, logits_ref, held_ref, out_ref, buffer, mass_ref, sem_in, sem_out):
    extent = logits_ref.shape[0]
    pieces = chunks_of(extent)
    loads = []
    for i, (start, size) in enumerate(pieces):
        where = pl.ds(start, size)
        load = pltpu.make_async_copy(anchors_ref.at[where], buffer.at[where], sem_in.at[i])
        load.start()
        loads.append(load)
    stores = []

    def anchors_of(start, size):
        i = start // CHUNK
        where = pl.ds(start, size)
        loads[i].wait()
        block = with_self(buffer[where, :], tokens_ref[...], start)
        buffer[where, :] = block
        store = pltpu.make_async_copy(buffer.at[where], held_ref.at[where], sem_out.at[i])
        store.start()
        stores.append(store)
        return buffer[where, :]

    put_masses(logits_ref, anchors_of, out_ref, mass_ref)
    for store in stores:
        store.wait()


def owner_kernel(full_vocab, target_pieces, in_ref, target_ref, out_ref, sum_ref=None):
    half = in_ref.shape[2] - LANES
    if target_pieces:
        target = jnp.sum(target_ref[...].astype(jnp.float32), axis=0)
        sum_ref[...] = target
    else:
        target = target_ref[...]
    stats = in_ref[:, :, half:].astype(jnp.float32)
    lane = lax.broadcasted_iota(jnp.int32, stats.shape, 2)
    top = jnp.sum(jnp.where(lane < 3, stats, 0.0), axis=2, keepdims=True)
    part = jnp.sum(jnp.where((lane >= 3) & (lane < 6), stats, 0.0), axis=2, keepdims=True)
    row_max = jnp.max(top, axis=0, keepdims=True)
    factor = jnp.exp(top - row_max)
    total = jnp.sum(part * factor, axis=0)
    mass = jnp.sum(in_ref[:, :, :half].astype(jnp.float32) * factor, axis=0)
    gap = full_vocab * mass / total - target
    sent = gap.astype(jnp.bfloat16)
    squares = jnp.sum(gap * gap, axis=1, keepdims=True)
    inner = jnp.sum(sent.astype(jnp.float32) * mass, axis=1, keepdims=True)
    lane = lax.broadcasted_iota(jnp.int32, (in_ref.shape[1], LANES), 1)
    tile = jnp.zeros((in_ref.shape[1], LANES), jnp.float32)
    parts = three_parts(row_max[0]) + three_parts(total) + three_parts(squares) + three_parts(inner)
    for i, value in enumerate(parts):
        tile = jnp.where(lane == i, value, tile)
    out_ref[:, :, :half] = jnp.broadcast_to(sent[None], (in_ref.shape[0],) + sent.shape)
    out_ref[:, :, half:] = jnp.broadcast_to(tile.astype(jnp.bfloat16)[None], (in_ref.shape[0],) + tile.shape)


def step_kernel(last, gap_ref, active_ref, base_ref, update_ref, held_ref, *rest):
    if last:
        new_ref, buffer, gap_all, sem_in = rest
    else:
        new_ref, out_ref, buffer, gap_all, logits_ref, mass_ref, sem_in = rest
    extent, rows = base_ref.shape
    loads = []
    for i, (start, size) in enumerate(chunks_of(extent)):
        where = pl.ds(start, size)
        load = pltpu.make_async_copy(held_ref.at[where], buffer.at[where], sem_in.at[i])
        load.start()
        loads.append(load)
    groups, halves, eight, width = gap_ref.shape
    half = width - LANES
    for h in range(halves):
        piece = gap_ref[:, h, :, :half].astype(jnp.float32).reshape(rows, half)
        gap_all[:, h * half : (h + 1) * half] = piece.astype(jnp.bfloat16)
    stats = [gap_ref[:, h, :, half:].astype(jnp.float32).reshape(rows, LANES).T for h in range(halves)]

    def joined(which, h):
        return jnp.sum(stats[h][3 * which : 3 * which + 3], axis=0, keepdims=True)

    row_max, total = joined(0, 0), joined(1, 0)
    squares = joined(2, 0) + joined(2, 1)
    inner = joined(3, 0) + joined(3, 1)
    scale = lax.rsqrt(squares / (halves * half) + epsilon)
    slope = scale * inner / total
    active = active_ref[...]
    for i, (start, size) in enumerate(chunks_of(extent)):
        where = pl.ds(start, size)
        loads[i].wait()
        back = matmul_nt(buffer[where, :], gap_all[...]) * scale
        logits = base_ref[where, :]
        if update_ref is not None:
            logits = logits + update_ref[where, :]
        weights = jnp.exp(logits - row_max)
        change = -step_size * active * weights * (back - slope)
        new_ref[where, :] = change if update_ref is None else update_ref[where, :] + change
        if not last:
            logits_ref[where, :] = logits + change
    if not last:
        put_masses(logits_ref, lambda start, size: buffer[pl.ds(start, size), :], out_ref, mass_ref)


def no_update(kernel):
    def run(gap_ref, active_ref, base_ref, held_ref, *rest):
        kernel(gap_ref, active_ref, base_ref, None, held_ref, *rest)

    return run


def target_kernel(core_ref, tokens_ref, delta_ref, anchors_ref, mine_ref, other_ref):
    extent, columns = anchors_ref.shape
    half = columns // 2
    delta = delta_ref[...]

    def product(which):
        where = pl.ds(pl.multiple_of(which * half, half), half)
        block = anchors_ref[:, where].astype(jnp.float32)
        place = lax.broadcasted_iota(jnp.int32, (extent, half), 0)
        block = jnp.where(place == tokens_ref[:, where], block + 1.0, block).astype(jnp.bfloat16)
        return jnp.dot(delta, block, preferred_element_type=jnp.float32)

    core = core_ref[0]
    other_ref[...] = product(1 - core).astype(jnp.bfloat16)
    mine_ref[...] = product(core)


def shards(expert_delta, small_anchors, small_tokens, base_logits, base_anchors, base_tokens, active_rows):
    f32, bf16 = jnp.float32, jnp.bfloat16
    vocab_count = lax.axis_size(VOCAB)
    vocab_place = lax.axis_index(VOCAB)
    place = lax.axis_index("rows") * vocab_count + vocab_place
    all_rows, small_width = expert_delta.shape
    base_width, anchors = base_anchors.shape
    rows = base_logits.shape[0]
    half = anchors // 2
    width = half + LANES
    eight = 2 * rows // vocab_count
    groups = vocab_count // 2
    pieces = len(chunks_of(base_width))
    params = pltpu.CompilerParams(vmem_limit_bytes=50 * 1024 * 1024)

    core = lax.axis_index("core").reshape(1)
    small_ids = (small_tokens - place * small_width)[None, :]
    shifted = base_tokens - vocab_place * base_width
    shifted = jnp.where((shifted >= 0) & (shifted < base_width), shifted, -1).astype(jnp.int16)
    base_ids = jnp.broadcast_to(shifted[None, :], (16, anchors))
    active = active_rows.astype(f32)[None, :]
    base = base_logits.T

    mine, other = pl.pallas_call(
        target_kernel,
        out_shape=(jax.ShapeDtypeStruct((all_rows, half), f32), jax.ShapeDtypeStruct((all_rows, half), bf16)),
        in_specs=[SMEM, VMEM, VMEM, VMEM],
        out_specs=(VMEM, VMEM),
        compiler_params=params,
        name="target_parts",
    )(core, small_ids, expert_delta, small_anchors)
    other = lax.ppermute(other, "core", [(0, 1), (1, 0)])
    target = (mine + other.astype(f32)).astype(bf16)
    target = target.reshape(-1, eight, half)
    target = lax.all_to_all(target, CHIPS, 0, 0, tiled=True)

    sent_shape = jax.ShapeDtypeStruct((groups, 2, eight, width), bf16)
    held_shape = jax.ShapeDtypeStruct((base_width, anchors), bf16)
    update_shape = jax.ShapeDtypeStruct((base_width, rows), f32)
    held, sent = pl.pallas_call(
        first_kernel,
        out_shape=(held_shape, sent_shape),
        in_specs=[VMEM, HBM, VMEM],
        out_specs=(HBM, VMEM),
        scratch_shapes=[
            pltpu.VMEM((base_width, anchors), bf16),
            pltpu.VMEM((rows, anchors), f32),
            pltpu.SemaphoreType.DMA((pieces,)),
            pltpu.SemaphoreType.DMA((pieces,)),
        ],
        compiler_params=params,
        name="first_masses",
    )(base_ids, base_anchors, base)

    update = None
    for turn in range(ITERATIONS):
        last = turn == ITERATIONS - 1
        got = lax.all_to_all(sent.reshape(vocab_count, eight, width), VOCAB, 0, 0, tiled=True)
        owner_shape = jax.ShapeDtypeStruct((vocab_count, eight, width), bf16)
        target_shape = jax.ShapeDtypeStruct((eight, half), f32)
        first = turn == 0
        result = pl.pallas_call(
            functools.partial(owner_kernel, float(base_width * vocab_count), first),
            out_shape=(owner_shape, target_shape) if first else owner_shape,
            in_specs=[VMEM, VMEM],
            out_specs=(VMEM, VMEM) if first else VMEM,
            compiler_params=params,
            name="owner",
        )(got, target)
        if first:
            copies, target = result
        else:
            copies = result
        gaps = lax.all_to_all(copies, VOCAB, 0, 0, tiled=True).reshape(groups, 2, eight, width)
        kernel = functools.partial(step_kernel, last)
        operands = [gaps, active, base] + ([] if update is None else [update]) + [held]
        result = pl.pallas_call(
            no_update(kernel) if update is None else kernel,
            out_shape=update_shape if last else (update_shape, sent_shape),
            in_specs=[VMEM] * (len(operands) - 1) + [HBM],
            out_specs=VMEM if last else (VMEM, VMEM),
            scratch_shapes=[pltpu.VMEM((base_width, anchors), bf16), pltpu.VMEM((rows, anchors), bf16)]
            + ([] if last else [pltpu.VMEM((base_width, rows), f32), pltpu.VMEM((rows, anchors), f32)])
            + [pltpu.SemaphoreType.DMA((pieces,))],
            compiler_params=params,
            name="step",
        )(*operands)
        if last:
            update = result
        else:
            update, sent = result
    return update.T


def solution(mesh):
    split = Mesh(mesh.devices.reshape(mesh.shape["rows"], 4, 4, 2), ("rows",) + VOCAB)
    everywhere = ("rows",) + VOCAB
    in_specs = (
        P(None, everywhere),
        P(everywhere, None),
        P(),
        P("rows", VOCAB),
        P(VOCAB, None),
        P(),
        P("rows"),
    )
    return jax.shard_map(shards, mesh=split, in_specs=in_specs, out_specs=P("rows", VOCAB), check_vma=False)
```

```python
import functools
import jax
import jax.numpy as jnp
from jax import lax
from jax.experimental import pallas as pl
from jax.experimental.pallas import tpu as pltpu
from jax.sharding import Mesh
from jax.sharding import PartitionSpec as P

ITERATIONS = 3
VOCAB = ("x", "y", "core")
CHIPS = ("rows", "x", "y")
LANES = 128
CHUNK = 512
AHEAD = 2
epsilon = 1e-06
step_size = 2.0

def grant(mebibytes):
    return pltpu.CompilerParams(vmem_limit_bytes=mebibytes * 1024 * 1024)


HBM = pl.BlockSpec(memory_space=pl.ANY)
VMEM = pl.BlockSpec(memory_space=pltpu.VMEM)
SMEM = pl.BlockSpec(memory_space=pltpu.SMEM)


def chunks_of(extent):
    starts = list(range(0, extent, CHUNK))
    return [(start, min(CHUNK, extent - start)) for start in starts]


def three_parts(value):
    high = value.astype(jnp.bfloat16).astype(jnp.float32)
    rest = value - high
    middle = rest.astype(jnp.bfloat16).astype(jnp.float32)
    return high, middle, rest - middle


def matmul_nt(left, right):
    return lax.dot_general(left, right, (((1,), (1,)), ((), ())), preferred_element_type=jnp.float32)


def with_self(block, tokens, start):
    rows, columns = block.shape
    if rows % 16 == 0:
        place = lax.broadcasted_iota(jnp.int16, (rows, columns), 0) + jnp.int16(start)
        wanted = jnp.broadcast_to(tokens[None], (rows // 16, 16, columns)).reshape(rows, columns)
    else:
        place = lax.broadcasted_iota(jnp.int16, (rows, columns), 0) + jnp.int16(start)
        whole = -(-rows // 16)
        wanted = jnp.broadcast_to(tokens[None], (whole, 16, columns)).reshape(whole * 16, columns)[:rows]
    return jnp.where(place == wanted, block + jnp.bfloat16(1), block)


def put_masses(core, logits_ref, anchors_of, mine_ref, other_ref, mass_ref):
    extent, rows = logits_ref.shape
    top = jnp.max(logits_ref[...], axis=0, keepdims=True)
    total = jnp.zeros((1, rows), jnp.float32)
    for start, size in chunks_of(extent):
        weights = jnp.exp(logits_ref[pl.ds(start, size), :] - top)
        total = total + jnp.sum(weights, axis=0, keepdims=True)
        turned = weights.T.astype(jnp.bfloat16)
        part = jnp.dot(turned, anchors_of(start, size), preferred_element_type=jnp.float32)
        if start == 0:
            mass_ref[...] = part
        else:
            mass_ref[...] += part
    groups, eight, width = mine_ref.shape
    half = width - LANES
    parts = three_parts(top) + three_parts(total)
    stats = jnp.concatenate(list(parts) + [jnp.zeros((LANES - len(parts), rows), jnp.float32)], axis=0)
    stats = stats.T.reshape(groups, eight, LANES).astype(jnp.bfloat16)
    for out_ref, which in ((mine_ref, core), (other_ref, 1 - core)):
        columns = pl.ds(pl.multiple_of(which * half, half), half)
        out_ref[:, :, :half] = mass_ref[:, columns].reshape(groups, eight, half).astype(jnp.bfloat16)
        out_ref[:, :, half:] = stats


def first_kernel(place_ref, tokens_ref, anchors_ref, logits_hbm, held_ref, mine_ref, other_ref, buffer, logits_ref, mass_ref, sem_in, sem_out, sem_base):
    extent, rows = logits_ref.shape
    base = pltpu.make_async_copy(logits_hbm, logits_ref, sem_base)
    base.start()
    loads, stores = [], []
    for i, (start, size) in enumerate(chunks_of(extent)):
        where = pl.ds(start, size)
        loads.append(pltpu.make_async_copy(anchors_ref.at[where], buffer.at[where], sem_in.at[i]))
    for load in loads[:AHEAD]:
        load.start()
    shifted = tokens_ref[...] - place_ref[0]
    shifted = jnp.where((shifted >= 0) & (shifted < extent), shifted, -1)
    tokens = jnp.broadcast_to(shifted, (16, shifted.shape[1])).astype(jnp.int16)
    base.wait()

    def anchors_of(start, size):
        i = start // CHUNK
        where = pl.ds(start, size)
        loads[i].wait()
        if i + AHEAD < len(loads):
            loads[i + AHEAD].start()
        buffer[where, :] = with_self(buffer[where, :], tokens, start)
        store = pltpu.make_async_copy(buffer.at[where], held_ref.at[where], sem_out.at[i])
        store.start()
        stores.append(store)
        return buffer[where, :]

    put_masses(place_ref[1], logits_ref, anchors_of, mine_ref, other_ref, mass_ref)
    for store in stores:
        store.wait()


def lane_sum(stats, which):
    lane = lax.broadcasted_iota(jnp.int32, stats.shape, stats.ndim - 1)
    chosen = (lane >= 3 * which) & (lane < 3 * which + 3)
    return jnp.sum(jnp.where(chosen, stats, 0.0), axis=-1, keepdims=True)


def lane_tile(shape, values):
    lane = lax.broadcasted_iota(jnp.int32, shape, len(shape) - 1)
    tile = jnp.zeros(shape, jnp.float32)
    for i, part in enumerate(part for value in values for part in three_parts(value)):
        tile = jnp.where(lane == i, part, tile)
    return tile.astype(jnp.bfloat16)


def pair_kernel(mine_ref, other_ref, out_ref):
    half = out_ref.shape[2] - LANES
    stats = [ref[:, :, half:].astype(jnp.float32) for ref in (mine_ref, other_ref)]
    tops = [lane_sum(stat, 0) for stat in stats]
    top = jnp.maximum(*tops)
    factors = [jnp.exp(each - top) for each in tops]
    total = sum(lane_sum(stat, 1) * factor for stat, factor in zip(stats, factors))
    mine = mine_ref[:, :, :half].astype(jnp.float32) * factors[0]
    other = other_ref[:, :, :half].astype(jnp.float32) * factors[1]
    out_ref[:, :, :half] = (mine + other).astype(jnp.bfloat16)
    out_ref[:, :, half:] = lane_tile(stats[0].shape, (top, total))


def owner_kernel(full_vocab, first, in_ref, target_ref, out_ref, sum_ref=None):
    half = in_ref.shape[2] - LANES
    if first:
        target = jnp.sum(target_ref[...].astype(jnp.float32), axis=0)
        sum_ref[...] = target
    else:
        target = target_ref[...]
    stats = in_ref[:, :, half:].astype(jnp.float32)
    top = lane_sum(stats, 0)
    row_max = jnp.max(top, axis=0, keepdims=True)
    factor = jnp.exp(top - row_max)
    total = jnp.sum(lane_sum(stats, 1) * factor, axis=0)
    mass = jnp.sum(in_ref[:, :, :half].astype(jnp.float32) * factor, axis=0)
    gap = full_vocab * mass / total - target
    sent = gap.astype(jnp.bfloat16)
    squares = jnp.sum(gap * gap, axis=1, keepdims=True)
    inner = jnp.sum(sent.astype(jnp.float32) * mass, axis=1, keepdims=True)
    tile = lane_tile((in_ref.shape[1], LANES), (row_max[0], total, squares, inner))
    out_ref[:, :, :half] = jnp.broadcast_to(sent[None], (in_ref.shape[0],) + sent.shape)
    out_ref[:, :, half:] = jnp.broadcast_to(tile[None], (in_ref.shape[0],) + tile.shape)


def step_kernel(last, place_ref, mine_gap_ref, other_gap_ref, active_ref, base_ref, update_ref, held_ref, *rest):
    if last:
        new_ref, gap_all = rest
    else:
        new_ref, mine_ref, other_ref, gap_all, logits_ref, mass_ref = rest
    extent, rows = base_ref.shape
    half = mine_gap_ref.shape[2] - LANES
    core = place_ref[1]
    stats = []
    for gap_ref, which in ((mine_gap_ref, core), (other_gap_ref, 1 - core)):
        columns = pl.ds(pl.multiple_of(which * half, half), half)
        piece = gap_ref[:, :, :half].astype(jnp.float32).reshape(rows, half)
        gap_all[:, columns] = piece.astype(jnp.bfloat16)
        stats.append(gap_ref[:, :, half:].astype(jnp.float32).reshape(rows, LANES).T)

    def joined(which, h):
        return jnp.sum(stats[h][3 * which : 3 * which + 3], axis=0, keepdims=True)

    row_max, total = joined(0, 0), joined(1, 0)
    squares = joined(2, 0) + joined(2, 1)
    inner = joined(3, 0) + joined(3, 1)
    scale = lax.rsqrt(squares / (2 * half) + epsilon)
    slope = scale * inner / total
    active = active_ref[...].astype(jnp.float32)
    for start, size in chunks_of(extent):
        where = pl.ds(start, size)
        back = matmul_nt(held_ref[where, :], gap_all[...]) * scale
        logits = base_ref[where, :]
        if update_ref is not None:
            logits = logits + update_ref[where, :]
        weights = jnp.exp(logits - row_max)
        change = -step_size * active * weights * (back - slope)
        new_ref[where, :] = change if update_ref is None else update_ref[where, :] + change
        if not last:
            logits_ref[where, :] = logits + change
    if not last:
        put_masses(core, logits_ref, lambda start, size: held_ref[pl.ds(start, size), :], mine_ref, other_ref, mass_ref)


def no_update(kernel):
    def run(place_ref, mine_gap_ref, other_gap_ref, active_ref, base_ref, held_ref, *rest):
        kernel(place_ref, mine_gap_ref, other_gap_ref, active_ref, base_ref, None, held_ref, *rest)

    return run


def target_kernel(place_ref, tokens_ref, *rest):
    out_ref = rest[-1]
    half = out_ref.shape[1]
    columns = pl.ds(pl.multiple_of(place_ref[0] * half, half), half)
    tokens = tokens_ref[:, columns]
    total = None
    for i in range(2):
        delta_ref, anchors_ref = rest[2 * i : 2 * i + 2]
        block = anchors_ref[:, columns].astype(jnp.float32)
        place = lax.broadcasted_iota(jnp.int32, block.shape, 0) + place_ref[1 + i]
        block = jnp.where(place == tokens, block + 1.0, block).astype(jnp.bfloat16)
        part = jnp.dot(delta_ref[...], block, preferred_element_type=jnp.float32)
        total = part if total is None else total + part
    out_ref[...] = total.astype(jnp.bfloat16)


def shards(expert_delta, small_anchors, small_tokens, base_logits, base_anchors, base_tokens, active_rows):
    f32, bf16 = jnp.float32, jnp.bfloat16
    vocab_count = lax.axis_size(VOCAB)
    vocab_place = lax.axis_index(VOCAB)
    place = lax.axis_index("rows") * vocab_count + vocab_place
    all_rows, small_width = expert_delta.shape
    base_width, anchors = base_anchors.shape
    rows = base_logits.shape[0]
    half = anchors // 2
    width = half + LANES
    eight = 2 * rows // vocab_count
    groups = vocab_count // 2
    pieces = len(chunks_of(base_width))

    core = lax.axis_index("core")
    small_place = jnp.stack([core, place * small_width, (place + 1 - 2 * core) * small_width])
    base_place = jnp.stack([vocab_place * base_width, core])
    small_tokens, base_tokens = small_tokens[None, :], base_tokens[None, :]
    active = active_rows[None, :]
    base = base_logits.T

    swap = [(0, 1), (1, 0)]
    other_delta = lax.ppermute(expert_delta, "core", swap)
    other_anchors = lax.ppermute(small_anchors, "core", swap)
    target = pl.pallas_call(
        target_kernel,
        out_shape=jax.ShapeDtypeStruct((all_rows, half), bf16),
        in_specs=[SMEM, VMEM, VMEM, VMEM, VMEM, VMEM],
        out_specs=VMEM,
        compiler_params=grant(16),
        name="target_parts",
    )(small_place, small_tokens, expert_delta, small_anchors, other_delta, other_anchors)
    target = lax.all_to_all(target.reshape(-1, eight, half), CHIPS, 0, 0, tiled=True)

    sent_shape = jax.ShapeDtypeStruct((groups, eight, width), bf16)
    held_shape = jax.ShapeDtypeStruct((base_width, anchors), bf16)
    update_shape = jax.ShapeDtypeStruct((base_width, rows), f32)
    held, mine, other = pl.pallas_call(
        first_kernel,
        out_shape=(held_shape, sent_shape, sent_shape),
        in_specs=[SMEM, VMEM, HBM, HBM],
        out_specs=(HBM, VMEM, VMEM),
        scratch_shapes=[
            pltpu.VMEM((base_width, anchors), bf16),
            pltpu.VMEM((base_width, rows), f32),
            pltpu.VMEM((rows, anchors), f32),
            pltpu.SemaphoreType.DMA((pieces,)),
            pltpu.SemaphoreType.DMA((pieces,)),
            pltpu.SemaphoreType.DMA,
        ],
        compiler_params=grant(36),
        name="first_masses",
    )(base_place, base_tokens, base_anchors, base)

    def both(mine, other):
        other = lax.ppermute(other, "core", swap)
        return pl.pallas_call(
            pair_kernel,
            out_shape=sent_shape,
            in_specs=[VMEM, VMEM],
            out_specs=VMEM,
            compiler_params=grant(4),
            name="pair",
        )(mine, other)

    sent, target = lax.optimization_barrier((both(mine, other), target))
    update = None
    for turn in range(ITERATIONS):
        last = turn == ITERATIONS - 1
        got = lax.all_to_all(sent, CHIPS[1:], 0, 0, tiled=True)
        target_shape = jax.ShapeDtypeStruct((eight, half), f32)
        first = turn == 0
        result = pl.pallas_call(
            functools.partial(owner_kernel, float(base_width * vocab_count), first),
            out_shape=(sent_shape, target_shape) if first else sent_shape,
            in_specs=[VMEM, VMEM],
            out_specs=(VMEM, VMEM) if first else VMEM,
            compiler_params=grant(4),
            cost_estimate=pl.CostEstimate(flops=20_000_000_000, bytes_accessed=40_000_000, transcendentals=0) if first else None,
            name="owner",
        )(got, target)
        if first:
            copies, target = result
        else:
            copies = result
        gaps = lax.all_to_all(copies, CHIPS[1:], 0, 0, tiled=True)
        other_gaps = lax.ppermute(gaps, "core", swap)
        kernel = functools.partial(step_kernel, last)
        operands = [base_place, gaps, other_gaps, active, base] + ([] if update is None else [update]) + [held]
        result = pl.pallas_call(
            no_update(kernel) if update is None else kernel,
            out_shape=update_shape if last else (update_shape, sent_shape, sent_shape),
            in_specs=[SMEM] + [VMEM] * (len(operands) - 1),
            out_specs=VMEM if last else (VMEM, VMEM, VMEM),
            scratch_shapes=[pltpu.VMEM((rows, anchors), bf16)]
            + ([] if last else [pltpu.VMEM((base_width, rows), f32), pltpu.VMEM((rows, anchors), f32)]),
            compiler_params=grant(16),
            name="step",
        )(*operands)
        if last:
            update = result
        else:
            update, mine, other = result
            sent = both(mine, other)
    return update.T


def solution(mesh):
    split = Mesh(mesh.devices.reshape(mesh.shape["rows"], 4, 4, 2), ("rows",) + VOCAB)
    everywhere = ("rows",) + VOCAB
    in_specs = (
        P(None, everywhere),
        P(everywhere, None),
        P(),
        P("rows", VOCAB),
        P(VOCAB, None),
        P(),
        P("rows"),
    )
    return jax.shard_map(shards, mesh=split, in_specs=in_specs, out_specs=P("rows", VOCAB), check_vma=False)
```

```python
import functools
import jax
import jax.numpy as jnp
from jax import lax
from jax.experimental import pallas as pl
from jax.experimental.pallas import tpu as pltpu
from jax.sharding import Mesh
from jax.sharding import PartitionSpec as P

ITERATIONS = 3
VOCAB = ("x", "y", "core")
CHIPS = ("rows", "x", "y")
LANES = 128
CHUNK = 512
AHEAD = 3
epsilon = 1e-06
step_size = 2.0


def grant(mebibytes):
    return pltpu.CompilerParams(vmem_limit_bytes=mebibytes * 1024 * 1024)


HBM = pl.BlockSpec(memory_space=pl.ANY)
VMEM = pl.BlockSpec(memory_space=pltpu.VMEM)
SMEM = pl.BlockSpec(memory_space=pltpu.SMEM)


def chunks_of(extent):
    starts = list(range(0, extent, CHUNK))
    return [(start, min(CHUNK, extent - start)) for start in starts]


def three_parts(value):
    high = value.astype(jnp.bfloat16).astype(jnp.float32)
    rest = value - high
    middle = rest.astype(jnp.bfloat16).astype(jnp.float32)
    return high, middle, rest - middle


def with_self(block, tokens, start):
    rows, columns = block.shape
    if rows % 16 == 0:
        place = lax.broadcasted_iota(jnp.int16, (rows, columns), 0) + jnp.int16(start)
        wanted = jnp.broadcast_to(tokens[None], (rows // 16, 16, columns)).reshape(rows, columns)
    else:
        place = lax.broadcasted_iota(jnp.int16, (rows, columns), 0) + jnp.int16(start)
        whole = -(-rows // 16)
        wanted = jnp.broadcast_to(tokens[None], (whole, 16, columns)).reshape(whole * 16, columns)[:rows]
    return jnp.where(place == wanted, block + jnp.bfloat16(1), block)


def put_masses(core, logits_ref, anchors_of, mine_ref, other_ref, mass_ref):
    extent, rows = logits_ref.shape
    top = jnp.max(logits_ref[...], axis=0, keepdims=True)
    total = jnp.zeros((1, rows), jnp.float32)
    for start, size in chunks_of(extent):
        weights = jnp.exp(logits_ref[pl.ds(start, size), :] - top)
        total = total + jnp.sum(weights, axis=0, keepdims=True)
        turned = weights.T.astype(jnp.bfloat16)
        part = jnp.dot(turned, anchors_of(start, size), preferred_element_type=jnp.float32)
        if start == 0:
            mass_ref[...] = part
        else:
            mass_ref[...] += part
    groups, eight, width = mine_ref.shape
    half = width - LANES
    parts = three_parts(top) + three_parts(total)
    stats = jnp.concatenate(list(parts) + [jnp.zeros((LANES - len(parts), rows), jnp.float32)], axis=0)
    stats = stats.T.reshape(groups, eight, LANES).astype(jnp.bfloat16)
    for out_ref, which in ((mine_ref, core), (other_ref, 1 - core)):
        columns = pl.ds(pl.multiple_of(which * half, half), half)
        out_ref[:, :, :half] = mass_ref[:, columns].reshape(groups, eight, half).astype(jnp.bfloat16)
        out_ref[:, :, half:] = stats


def first_kernel(place_ref, tokens_ref, anchors_ref, logits_hbm, held_ref, turned_ref, mine_ref, other_ref, logits_ref, mass_ref, sems, sem_base):
    extent = logits_ref.shape[0]
    base = pltpu.make_async_copy(logits_hbm, logits_ref, sem_base)
    base.start()
    loads = []
    for i, (start, size) in enumerate(chunks_of(extent)):
        where = pl.ds(start, size)
        loads.append(pltpu.make_async_copy(anchors_ref.at[where], held_ref.at[where], sems.at[i]))
    for load in loads[:AHEAD]:
        load.start()
    shifted = tokens_ref[...] - place_ref[0]
    shifted = jnp.where((shifted >= 0) & (shifted < extent), shifted, -1)
    tokens = jnp.broadcast_to(shifted, (16, shifted.shape[1])).astype(jnp.int16)
    base.wait()

    def anchors_of(start, size):
        i = start // CHUNK
        where = pl.ds(start, size)
        loads[i].wait()
        if i + AHEAD < len(loads):
            loads[i + AHEAD].start()
        block = with_self(held_ref[where, :], tokens, start)
        held_ref[where, :] = block
        turned_ref[:, start : start + size] = block.T
        return held_ref[where, :]

    put_masses(place_ref[1], logits_ref, anchors_of, mine_ref, other_ref, mass_ref)


def lane_sum(stats, which):
    lane = lax.broadcasted_iota(jnp.int32, stats.shape, stats.ndim - 1)
    chosen = (lane >= 3 * which) & (lane < 3 * which + 3)
    return jnp.sum(jnp.where(chosen, stats, 0.0), axis=-1, keepdims=True)


def lane_tile(shape, values):
    lane = lax.broadcasted_iota(jnp.int32, shape, len(shape) - 1)
    tile = jnp.zeros(shape, jnp.float32)
    for i, part in enumerate(part for value in values for part in three_parts(value)):
        tile = jnp.where(lane == i, part, tile)
    return tile.astype(jnp.bfloat16)


def pair_kernel(mine_ref, other_ref, *rest):
    out_ref = rest[-1]
    groups, eight, width = mine_ref.shape
    half = width - LANES
    if len(rest) > 1:
        target = sum(ref[...].astype(jnp.float32) for ref in rest[:-1])
        out_ref[:, :, width:] = target.reshape(groups, eight, half).astype(jnp.bfloat16)
    stats = [ref[:, :, half:].astype(jnp.float32) for ref in (mine_ref, other_ref)]
    tops = [lane_sum(stat, 0) for stat in stats]
    top = jnp.maximum(*tops)
    factors = [jnp.exp(each - top) for each in tops]
    total = sum(lane_sum(stat, 1) * factor for stat, factor in zip(stats, factors))
    mine = mine_ref[:, :, :half].astype(jnp.float32) * factors[0]
    other = other_ref[:, :, :half].astype(jnp.float32) * factors[1]
    out_ref[:, :, :half] = (mine + other).astype(jnp.bfloat16)
    out_ref[:, :, half:width] = lane_tile(stats[0].shape, (top, total))


def owner_kernel(full_vocab, first, in_ref, *rest):
    if first:
        out_ref, sum_ref = rest
    else:
        target_ref, out_ref = rest
    width = out_ref.shape[2]
    half = width - LANES
    if first:
        target = jnp.sum(in_ref[:, :, width:].astype(jnp.float32), axis=0)
        sum_ref[...] = target
    else:
        target = target_ref[...]
    stats = in_ref[:, :, half:width].astype(jnp.float32)
    top = lane_sum(stats, 0)
    row_max = jnp.max(top, axis=0, keepdims=True)
    factor = jnp.exp(top - row_max)
    total = jnp.sum(lane_sum(stats, 1) * factor, axis=0)
    mass = jnp.sum(in_ref[:, :, :half].astype(jnp.float32) * factor, axis=0)
    gap = full_vocab * mass / total - target
    sent = gap.astype(jnp.bfloat16)
    squares = jnp.sum(gap * gap, axis=1, keepdims=True)
    inner = jnp.sum(sent.astype(jnp.float32) * mass, axis=1, keepdims=True)
    tile = lane_tile((in_ref.shape[1], LANES), (row_max[0], total, squares, inner))
    out_ref[:, :, :half] = jnp.broadcast_to(sent[None], (in_ref.shape[0],) + sent.shape)
    out_ref[:, :, half:] = jnp.broadcast_to(tile[None], (in_ref.shape[0],) + tile.shape)


def step_kernel(last, place_ref, mine_gap_ref, other_gap_ref, active_ref, base_ref, update_ref, turned_ref, *rest):
    if last:
        new_ref, gap_all = rest
    else:
        held_ref, new_ref, mine_ref, other_ref, gap_all, logits_ref, mass_ref = rest
    extent, rows = base_ref.shape
    half = mine_gap_ref.shape[2] - LANES
    core = place_ref[1]
    stats = []
    for gap_ref, which in ((mine_gap_ref, core), (other_gap_ref, 1 - core)):
        columns = pl.ds(pl.multiple_of(which * half, half), half)
        piece = gap_ref[:, :, :half].astype(jnp.float32).reshape(rows, half)
        gap_all[:, columns] = piece.astype(jnp.bfloat16)
        stats.append(gap_ref[:, :, half:].astype(jnp.float32).reshape(rows, LANES).T)

    def joined(which, h):
        return jnp.sum(stats[h][3 * which : 3 * which + 3], axis=0, keepdims=True)

    row_max, total = joined(0, 0), joined(1, 0)
    squares = joined(2, 0) + joined(2, 1)
    inner = joined(3, 0) + joined(3, 1)
    scale = lax.rsqrt(squares / (2 * half) + epsilon)
    slope = scale * inner / total
    active = active_ref[...].astype(jnp.float32)
    for start, size in chunks_of(extent):
        where = pl.ds(start, size)
        turned = jnp.dot(gap_all[...], turned_ref[:, start : start + size], preferred_element_type=jnp.float32)
        back = turned.T * scale
        logits = base_ref[where, :]
        if update_ref is not None:
            logits = logits + update_ref[where, :]
        weights = jnp.exp(logits - row_max)
        change = -step_size * active * weights * (back - slope)
        new_ref[where, :] = change if update_ref is None else update_ref[where, :] + change
        if not last:
            logits_ref[where, :] = logits + change
    if not last:
        put_masses(core, logits_ref, lambda start, size: held_ref[pl.ds(start, size), :], mine_ref, other_ref, mass_ref)


def no_update(kernel):
    def run(place_ref, mine_gap_ref, other_gap_ref, active_ref, base_ref, turned_ref, *rest):
        kernel(place_ref, mine_gap_ref, other_gap_ref, active_ref, base_ref, None, turned_ref, *rest)

    return run


def target_kernel(place_ref, *rest):
    *rest, total_ref, sems = rest
    sources, outs, (tokens_ref, *buffers) = rest[:5], rest[5:-5], rest[-5:]
    copies = [
        pltpu.make_async_copy(source, buffer, sems.at[i])
        for i, (source, buffer) in enumerate(zip(sources, (tokens_ref, *buffers)))
    ]
    for copy in copies:
        copy.start()
    rows, half = outs[0].shape
    columns = pl.ds(pl.multiple_of(place_ref[0] * half, half), half)
    copies[0].wait()
    tokens = tokens_ref[:, columns]
    total = None
    for i in range(2):
        for copy in copies[1 + 2 * i : 3 + 2 * i]:
            copy.wait()
        delta_ref, anchors_ref = buffers[2 * i : 2 * i + 2]
        block = anchors_ref[:, columns].astype(jnp.float32)
        place = lax.broadcasted_iota(jnp.int32, block.shape, 0) + place_ref[1 + i]
        block = jnp.where(place == tokens, block + 1.0, block).astype(jnp.bfloat16)
        part = jnp.dot(delta_ref[...], block, preferred_element_type=jnp.float32)
        total = part if total is None else total + part
    total_ref[...] = total
    for far, out_ref in enumerate(outs):
        group = lax.rem(place_ref[3] + far, len(outs))
        out_ref[...] = total_ref[pl.ds(pl.multiple_of(group * rows, rows), rows), :].astype(jnp.bfloat16)


def shards(expert_delta, small_anchors, small_tokens, base_logits, base_anchors, base_tokens, active_rows):
    f32, bf16 = jnp.float32, jnp.bfloat16
    vocab_count = lax.axis_size(VOCAB)
    vocab_place = lax.axis_index(VOCAB)
    place = lax.axis_index("rows") * vocab_count + vocab_place
    all_rows, small_width = expert_delta.shape
    base_width, anchors = base_anchors.shape
    rows = base_logits.shape[0]
    half = anchors // 2
    width = half + LANES
    eight = 2 * rows // vocab_count
    groups = vocab_count // 2
    pieces = len(chunks_of(base_width))

    core = lax.axis_index("core")
    small_place = jnp.stack([core, place * small_width, (place + 1 - 2 * core) * small_width, lax.axis_index("rows")])
    base_place = jnp.stack([vocab_place * base_width, core])
    small_tokens, base_tokens = small_tokens[None, :], base_tokens[None, :]
    active = active_rows[None, :]
    base = base_logits.T

    swap = [(0, 1), (1, 0)]
    other_delta = lax.ppermute(expert_delta, "core", swap)
    other_anchors = lax.ppermute(small_anchors, "core", swap)
    row_groups = lax.axis_size("rows")
    targets = pl.pallas_call(
        target_kernel,
        out_shape=(jax.ShapeDtypeStruct((rows, half), bf16),) * row_groups,
        in_specs=[SMEM] + [HBM] * 5,
        out_specs=(VMEM,) * row_groups,
        scratch_shapes=[pltpu.VMEM(small_tokens.shape, jnp.int32)]
        + [pltpu.VMEM(each.shape, bf16) for each in (expert_delta, small_anchors)] * 2
        + [pltpu.VMEM((all_rows, half), f32), pltpu.SemaphoreType.DMA((5,))],
        compiler_params=grant(20),
        name="target_parts",
    )(
        small_place,
        *(pltpu.with_memory_space_constraint(each, pltpu.HBM) for each in (small_tokens, expert_delta, small_anchors)),
        other_delta,
        other_anchors,
    )
    base_place, base_tokens, targets = lax.optimization_barrier((base_place, base_tokens, list(targets)))
    for far in range(1, row_groups):
        ring = [(i, (i + far) % row_groups) for i in range(row_groups)]
        targets[far] = lax.ppermute(targets[far], "rows", ring)

    sent_shape = jax.ShapeDtypeStruct((groups, eight, width), bf16)
    held_shape = pltpu.VMEM((base_width, anchors), bf16)
    turned_shape = pltpu.VMEM((anchors, -(-base_width // LANES) * LANES), bf16)
    update_shape = jax.ShapeDtypeStruct((base_width, rows), f32)
    held, turned, mine, other = pl.pallas_call(
        first_kernel,
        out_shape=(held_shape, turned_shape, sent_shape, sent_shape),
        in_specs=[SMEM, VMEM, HBM, HBM],
        out_specs=(VMEM,) * 4,
        scratch_shapes=[
            pltpu.VMEM((base_width, rows), f32),
            pltpu.VMEM((rows, anchors), f32),
            pltpu.SemaphoreType.DMA((pieces,)),
            pltpu.SemaphoreType.DMA,
        ],
        compiler_params=grant(23),
        cost_estimate=pl.CostEstimate(flops=8_000_000_000, bytes_accessed=40_000_000, transcendentals=base_width * rows),
        name="first_masses",
    )(base_place, base_tokens, base_anchors, base)

    def both(mine, other, *more):
        other = lax.ppermute(other, "core", swap)
        return pl.pallas_call(
            pair_kernel,
            out_shape=jax.ShapeDtypeStruct((groups, eight, width + (half if more else 0)), bf16),
            in_specs=[VMEM] * (2 + len(more)),
            out_specs=VMEM,
            compiler_params=grant(5),
            name="pair",
        )(mine, other, *more)

    sent = both(mine, other, *targets)
    update = None
    for turn in range(ITERATIONS):
        last = turn == ITERATIONS - 1
        got = lax.all_to_all(sent, CHIPS[1:], 0, 0, tiled=True)
        target_shape = jax.ShapeDtypeStruct((eight, half), f32)
        first = turn == 0
        result = pl.pallas_call(
            functools.partial(owner_kernel, float(base_width * vocab_count), first),
            out_shape=(sent_shape, target_shape) if first else sent_shape,
            in_specs=[VMEM] if first else [VMEM, VMEM],
            out_specs=(VMEM, VMEM) if first else VMEM,
            compiler_params=grant(4),
            name="owner",
        )(*((got,) if first else (got, target)))
        if first:
            copies, target = result
        else:
            copies = result
        gaps = lax.all_to_all(copies, CHIPS[1:], 0, 0, tiled=True)
        other_gaps = lax.ppermute(gaps, "core", swap)
        kernel = functools.partial(step_kernel, last)
        operands = [base_place, gaps, other_gaps, active, base] + ([] if update is None else [update]) + [turned] + ([] if last else [held])
        result = pl.pallas_call(
            no_update(kernel) if update is None else kernel,
            out_shape=update_shape if last else (update_shape, sent_shape, sent_shape),
            in_specs=[SMEM] + [VMEM] * (len(operands) - 1),
            out_specs=VMEM if last else (VMEM, VMEM, VMEM),
            scratch_shapes=[pltpu.VMEM((rows, anchors), bf16)]
            + ([] if last else [pltpu.VMEM((base_width, rows), f32), pltpu.VMEM((rows, anchors), f32)]),
            compiler_params=grant(7),
            name="step",
        )(*operands)
        if last:
            update = result
        else:
            update, mine, other = result
            sent = both(mine, other)
    return update.T


def solution(mesh):
    split = Mesh(mesh.devices.reshape(mesh.shape["rows"], 4, 4, 2), ("rows",) + VOCAB)
    everywhere = ("rows",) + VOCAB
    in_specs = (
        P(None, everywhere),
        P(everywhere, None),
        P(),
        P("rows", VOCAB),
        P(VOCAB, None),
        P(),
        P("rows"),
    )

    return jax.shard_map(shards, mesh=split, in_specs=in_specs, out_specs=P("rows", VOCAB), check_vma=False)
```

```python
import functools
import jax
import jax.numpy as jnp
from jax import lax
from jax.experimental import pallas as pl
from jax.experimental.pallas import tpu as pltpu
from jax.sharding import Mesh
from jax.sharding import PartitionSpec as P

ITERATIONS = 3
VOCAB = ("x", "y", "core")
CHIPS = ("rows", "x", "y")
LANES = 128
CHUNK = 512
AHEAD = 3
epsilon = 1e-06
step_size = 2.0


def grant(mebibytes):
    return pltpu.CompilerParams(vmem_limit_bytes=mebibytes * 1024 * 1024)


HBM = pl.BlockSpec(memory_space=pl.ANY)
VMEM = pl.BlockSpec(memory_space=pltpu.VMEM)
SMEM = pl.BlockSpec(memory_space=pltpu.SMEM)


def chunks_of(extent):
    starts = list(range(0, extent, CHUNK))
    return [(start, min(CHUNK, extent - start)) for start in starts]


def three_parts(value):
    high = value.astype(jnp.bfloat16).astype(jnp.float32)
    rest = value - high
    middle = rest.astype(jnp.bfloat16).astype(jnp.float32)
    return high, middle, rest - middle


def with_self(block, tokens, start):
    rows, columns = block.shape
    if rows % 16 == 0:
        place = lax.broadcasted_iota(jnp.int16, (rows, columns), 0) + jnp.int16(start)
        wanted = jnp.broadcast_to(tokens[None], (rows // 16, 16, columns)).reshape(rows, columns)
    else:
        place = lax.broadcasted_iota(jnp.int16, (rows, columns), 0) + jnp.int16(start)
        whole = -(-rows // 16)
        wanted = jnp.broadcast_to(tokens[None], (whole, 16, columns)).reshape(whole * 16, columns)[:rows]
    return jnp.where(place == wanted, block + jnp.bfloat16(1), block)


def put_masses(core, logits_ref, anchors_of, mine_ref, other_ref, mass_ref):
    extent, rows = logits_ref.shape
    top = jnp.max(logits_ref[...], axis=0, keepdims=True)
    total = jnp.zeros((1, rows), jnp.float32)
    for start, size in chunks_of(extent):
        weights = jnp.exp(logits_ref[pl.ds(start, size), :] - top)
        total = total + jnp.sum(weights, axis=0, keepdims=True)
        turned = weights.T.astype(jnp.bfloat16)
        part = jnp.dot(turned, anchors_of(start, size), preferred_element_type=jnp.float32)
        if start == 0:
            mass_ref[...] = part
        else:
            mass_ref[...] += part
    groups, eight, width = mine_ref.shape
    half = width - LANES
    parts = three_parts(top) + three_parts(total)
    stats = jnp.concatenate(list(parts) + [jnp.zeros((LANES - len(parts), rows), jnp.float32)], axis=0)
    stats = stats.T.reshape(groups, eight, LANES).astype(jnp.bfloat16)
    for out_ref, which in ((mine_ref, core), (other_ref, 1 - core)):
        columns = pl.ds(pl.multiple_of(which * half, half), half)
        out_ref[:, :, :half] = mass_ref[:, columns].reshape(groups, eight, half).astype(jnp.bfloat16)
        out_ref[:, :, half:] = stats


def first_kernel(place_ref, tokens_ref, anchors_ref, logits_ref, held_ref, turned_ref, mine_ref, other_ref, mass_ref, sems):
    extent = logits_ref.shape[0]
    loads = []
    for i, (start, size) in enumerate(chunks_of(extent)):
        where = pl.ds(start, size)
        loads.append(pltpu.make_async_copy(anchors_ref.at[where], held_ref.at[where], sems.at[i]))
    for load in loads[:AHEAD]:
        load.start()
    shifted = tokens_ref[...] - place_ref[0]
    shifted = jnp.where((shifted >= 0) & (shifted < extent), shifted, -1)
    tokens = jnp.broadcast_to(shifted, (16, shifted.shape[1])).astype(jnp.int16)

    def anchors_of(start, size):
        i = start // CHUNK
        where = pl.ds(start, size)
        loads[i].wait()
        if i + AHEAD < len(loads):
            loads[i + AHEAD].start()
        block = with_self(held_ref[where, :], tokens, start)
        held_ref[where, :] = block
        turned_ref[:, start : start + size] = block.T
        return held_ref[where, :]

    put_masses(place_ref[1], logits_ref, anchors_of, mine_ref, other_ref, mass_ref)


def lane_sum(stats, which):
    lane = lax.broadcasted_iota(jnp.int32, stats.shape, stats.ndim - 1)
    chosen = (lane >= 3 * which) & (lane < 3 * which + 3)
    return jnp.sum(jnp.where(chosen, stats, 0.0), axis=-1, keepdims=True)


def lane_tile(shape, values):
    lane = lax.broadcasted_iota(jnp.int32, shape, len(shape) - 1)
    tile = jnp.zeros(shape, jnp.float32)
    for i, part in enumerate(part for value in values for part in three_parts(value)):
        tile = jnp.where(lane == i, part, tile)
    return tile.astype(jnp.bfloat16)


def pair_kernel(mine_ref, other_ref, *rest):
    out_ref = rest[-1]
    groups, eight, width = mine_ref.shape
    half = width - LANES
    if len(rest) > 1:
        target = sum(ref[...].astype(jnp.float32) for ref in rest[:-1])
        out_ref[:, :, width:] = target.reshape(groups, eight, half).astype(jnp.bfloat16)
    stats = [ref[:, :, half:].astype(jnp.float32) for ref in (mine_ref, other_ref)]
    tops = [lane_sum(stat, 0) for stat in stats]
    top = jnp.maximum(*tops)
    factors = [jnp.exp(each - top) for each in tops]
    total = sum(lane_sum(stat, 1) * factor for stat, factor in zip(stats, factors))
    mine = mine_ref[:, :, :half].astype(jnp.float32) * factors[0]
    other = other_ref[:, :, :half].astype(jnp.float32) * factors[1]
    out_ref[:, :, :half] = (mine + other).astype(jnp.bfloat16)
    out_ref[:, :, half:width] = lane_tile(stats[0].shape, (top, total))


def owner_kernel(full_vocab, first, in_ref, *rest):
    if first:
        out_ref, sum_ref = rest
    else:
        target_ref, out_ref = rest
    width = out_ref.shape[2]
    half = width - LANES
    if first:
        target = jnp.sum(in_ref[:, :, width:].astype(jnp.float32), axis=0)
        sum_ref[...] = target
    else:
        target = target_ref[...]
    stats = in_ref[:, :, half:width].astype(jnp.float32)
    top = lane_sum(stats, 0)
    row_max = jnp.max(top, axis=0, keepdims=True)
    factor = jnp.exp(top - row_max)
    total = jnp.sum(lane_sum(stats, 1) * factor, axis=0)
    mass = jnp.sum(in_ref[:, :, :half].astype(jnp.float32) * factor, axis=0)
    gap = full_vocab * mass / total - target
    sent = gap.astype(jnp.bfloat16)
    squares = jnp.sum(gap * gap, axis=1, keepdims=True)
    inner = jnp.sum(sent.astype(jnp.float32) * mass, axis=1, keepdims=True)
    tile = lane_tile((in_ref.shape[1], LANES), (row_max[0], total, squares, inner))
    out_ref[:, :, :half] = jnp.broadcast_to(sent[None], (in_ref.shape[0],) + sent.shape)
    out_ref[:, :, half:] = jnp.broadcast_to(tile[None], (in_ref.shape[0],) + tile.shape)


def step_kernel(last, place_ref, mine_gap_ref, other_gap_ref, active_ref, base_ref, update_ref, turned_ref, *rest):
    if last:
        out_ref, new_ref, gap_all, sems = rest
    else:
        held_ref, new_ref, mine_ref, other_ref, gap_all, logits_ref, mass_ref = rest
    extent, rows = base_ref.shape
    half = mine_gap_ref.shape[2] - LANES
    core = place_ref[1]
    stats = []
    for gap_ref, which in ((mine_gap_ref, core), (other_gap_ref, 1 - core)):
        columns = pl.ds(pl.multiple_of(which * half, half), half)
        piece = gap_ref[:, :, :half].astype(jnp.float32).reshape(rows, half)
        gap_all[:, columns] = piece.astype(jnp.bfloat16)
        stats.append(gap_ref[:, :, half:].astype(jnp.float32).reshape(rows, LANES).T)

    def joined(which, h):
        return jnp.sum(stats[h][3 * which : 3 * which + 3], axis=0, keepdims=True)

    row_max, total = joined(0, 0), joined(1, 0)
    squares = joined(2, 0) + joined(2, 1)
    inner = joined(3, 0) + joined(3, 1)
    scale = lax.rsqrt(squares / (2 * half) + epsilon)
    slope = scale * inner / total
    active = active_ref[...].astype(jnp.float32)
    copies = []
    for start, size in chunks_of(extent):
        where = pl.ds(start, size)
        turned = jnp.dot(gap_all[...], turned_ref[:, start : start + size], preferred_element_type=jnp.float32)
        back = turned.T * scale
        logits = base_ref[where, :]
        if update_ref is not None:
            logits = logits + update_ref[where, :]
        weights = jnp.exp(logits - row_max)
        change = -step_size * active * weights * (back - slope)
        new_ref[where, :] = change if update_ref is None else update_ref[where, :] + change
        if last:
            copy = pltpu.make_async_copy(new_ref.at[where], out_ref.at[where], sems.at[len(copies)])
            copy.start()
            copies.append(copy)
        else:
            logits_ref[where, :] = logits + change
    for copy in copies:
        copy.wait()
    if not last:
        put_masses(core, logits_ref, lambda start, size: held_ref[pl.ds(start, size), :], mine_ref, other_ref, mass_ref)


def no_update(kernel):
    def run(place_ref, mine_gap_ref, other_gap_ref, active_ref, base_ref, turned_ref, *rest):
        kernel(place_ref, mine_gap_ref, other_gap_ref, active_ref, base_ref, None, turned_ref, *rest)

    return run


def target_kernel(place_ref, *rest):
    *rest, total_ref, sems = rest
    sources, outs, (tokens_ref, *buffers) = rest[:5], rest[5:-5], rest[-5:]
    copies = [
        pltpu.make_async_copy(source, buffer, sems.at[i])
        for i, (source, buffer) in enumerate(zip(sources, (tokens_ref, *buffers)))
    ]
    for copy in copies:
        copy.start()
    rows, half = outs[0].shape
    columns = pl.ds(pl.multiple_of(place_ref[0] * half, half), half)
    copies[0].wait()
    tokens = tokens_ref[:, columns]
    total = None
    for i in range(2):
        for copy in copies[1 + 2 * i : 3 + 2 * i]:
            copy.wait()
        delta_ref, anchors_ref = buffers[2 * i : 2 * i + 2]
        block = anchors_ref[:, columns].astype(jnp.float32)
        place = lax.broadcasted_iota(jnp.int32, block.shape, 0) + place_ref[1 + i]
        block = jnp.where(place == tokens, block + 1.0, block).astype(jnp.bfloat16)
        part = jnp.dot(delta_ref[...], block, preferred_element_type=jnp.float32)
        total = part if total is None else total + part
    total_ref[...] = total
    for far, out_ref in enumerate(outs):
        group = lax.rem(place_ref[3] + far, len(outs))
        out_ref[...] = total_ref[pl.ds(pl.multiple_of(group * rows, rows), rows), :].astype(jnp.bfloat16)


def shards(expert_delta, small_anchors, small_tokens, base_logits, base_anchors, base_tokens, active_rows):
    f32, bf16 = jnp.float32, jnp.bfloat16
    vocab_count = lax.axis_size(VOCAB)
    vocab_place = lax.axis_index(VOCAB)
    place = lax.axis_index("rows") * vocab_count + vocab_place
    all_rows, small_width = expert_delta.shape
    base_width, anchors = base_anchors.shape
    rows = base_logits.shape[0]
    half = anchors // 2
    width = half + LANES
    eight = 2 * rows // vocab_count
    groups = vocab_count // 2
    pieces = len(chunks_of(base_width))

    core = lax.axis_index("core")
    small_place = jnp.stack([core, place * small_width, (place + 1 - 2 * core) * small_width, lax.axis_index("rows")])
    base_place = jnp.stack([vocab_place * base_width, core])
    small_tokens, base_tokens = small_tokens[None, :], base_tokens[None, :]
    active = active_rows[None, :]
    base = base_logits.T

    swap = [(0, 1), (1, 0)]
    other_delta = lax.ppermute(expert_delta, "core", swap)
    other_anchors = lax.ppermute(small_anchors, "core", swap)
    row_groups = lax.axis_size("rows")
    targets = pl.pallas_call(
        target_kernel,
        out_shape=(jax.ShapeDtypeStruct((rows, half), bf16),) * row_groups,
        in_specs=[SMEM] + [HBM] * 5,
        out_specs=(VMEM,) * row_groups,
        scratch_shapes=[pltpu.VMEM(small_tokens.shape, jnp.int32)]
        + [pltpu.VMEM(each.shape, bf16) for each in (expert_delta, small_anchors)] * 2
        + [pltpu.VMEM((all_rows, half), f32), pltpu.SemaphoreType.DMA((5,))],
        compiler_params=grant(20),
        name="target_parts",
    )(
        small_place,
        *(pltpu.with_memory_space_constraint(each, pltpu.HBM) for each in (small_tokens, expert_delta, small_anchors)),
        other_delta,
        other_anchors,
    )
    base_place, base_tokens, targets = lax.optimization_barrier((base_place, base_tokens, list(targets)))
    for far in range(1, row_groups):
        ring = [(i, (i + far) % row_groups) for i in range(row_groups)]
        targets[far] = lax.ppermute(targets[far], "rows", ring)

    sent_shape = jax.ShapeDtypeStruct((groups, eight, width), bf16)
    held_shape = pltpu.VMEM((base_width, anchors), bf16)
    turned_shape = pltpu.VMEM((anchors, -(-base_width // LANES) * LANES), bf16)
    update_shape = jax.ShapeDtypeStruct((base_width, rows), f32)
    held, turned, mine, other = pl.pallas_call(
        first_kernel,
        out_shape=(held_shape, turned_shape, sent_shape, sent_shape),
        in_specs=[SMEM, VMEM, HBM, VMEM],
        out_specs=(VMEM,) * 4,
        scratch_shapes=[
            pltpu.VMEM((rows, anchors), f32),
            pltpu.SemaphoreType.DMA((pieces,)),
        ],
        compiler_params=grant(8),
        cost_estimate=pl.CostEstimate(flops=8_000_000_000, bytes_accessed=40_000_000, transcendentals=base_width * rows),
        name="first_masses",
    )(base_place, base_tokens, pltpu.with_memory_space_constraint(base_anchors, pltpu.HBM), base)

    def both(mine, other, *more):
        other = lax.ppermute(other, "core", swap)
        return pl.pallas_call(
            pair_kernel,
            out_shape=jax.ShapeDtypeStruct((groups, eight, width + (half if more else 0)), bf16),
            in_specs=[VMEM] * (2 + len(more)),
            out_specs=VMEM,
            compiler_params=grant(5),
            name="pair",
        )(mine, other, *more)

    sent = both(mine, other, *targets)
    update = None
    for turn in range(ITERATIONS):
        last = turn == ITERATIONS - 1
        got = lax.all_to_all(sent, CHIPS[1:], 0, 0, tiled=True)
        target_shape = jax.ShapeDtypeStruct((eight, half), f32)
        first = turn == 0
        result = pl.pallas_call(
            functools.partial(owner_kernel, float(base_width * vocab_count), first),
            out_shape=(sent_shape, target_shape) if first else sent_shape,
            in_specs=[VMEM] if first else [VMEM, VMEM],
            out_specs=(VMEM, VMEM) if first else VMEM,
            compiler_params=grant(4),
            name="owner",
        )(*((got,) if first else (got, target)))
        if first:
            copies, target = result
        else:
            copies = result
        gaps = lax.all_to_all(copies, CHIPS[1:], 0, 0, tiled=True)
        other_gaps = lax.ppermute(gaps, "core", swap)
        kernel = functools.partial(step_kernel, last)
        operands = [base_place, gaps, other_gaps, active, base] + ([] if update is None else [update]) + [turned] + ([] if last else [held])
        result = pl.pallas_call(
            no_update(kernel) if update is None else kernel,
            out_shape=update_shape if last else (update_shape, sent_shape, sent_shape),
            in_specs=[SMEM] + [VMEM] * (len(operands) - 1),
            out_specs=HBM if last else (VMEM, VMEM, VMEM),
            scratch_shapes=([pltpu.VMEM((base_width, rows), f32)] if last else [])
            + [pltpu.VMEM((rows, anchors), bf16)]
            + (
                [pltpu.SemaphoreType.DMA((pieces,))]
                if last
                else [pltpu.VMEM((base_width, rows), f32), pltpu.VMEM((rows, anchors), f32)]
            ),
            compiler_params=grant(7),
            name="step",
        )(*operands)
        if last:
            update = result
        else:
            update, mine, other = result
            sent = both(mine, other)
    return update.T


def solution(mesh):
    split = Mesh(mesh.devices.reshape(mesh.shape["rows"], 4, 4, 2), ("rows",) + VOCAB)
    everywhere = ("rows",) + VOCAB
    in_specs = (
        P(None, everywhere),
        P(everywhere, None),
        P(),
        P("rows", VOCAB),
        P(VOCAB, None),
        P(),
        P("rows"),
    )

    return jax.shard_map(shards, mesh=split, in_specs=in_specs, out_specs=P("rows", VOCAB), check_vma=False)
```

```python
import functools
import jax
import jax.numpy as jnp
from jax import lax
from jax.experimental import pallas as pl
from jax.experimental.pallas import tpu as pltpu
from jax.sharding import Mesh
from jax.sharding import PartitionSpec as P

ITERATIONS = 3
VOCAB = ("x", "y", "core")
CHIPS = ("rows", "x", "y")
LANES = 128
CHUNK = 512
AHEAD = 3
epsilon = 1e-06
step_size = 2.0


def grant(mebibytes):
    return pltpu.CompilerParams(vmem_limit_bytes=mebibytes * 1024 * 1024)


HBM = pl.BlockSpec(memory_space=pl.ANY)
VMEM = pl.BlockSpec(memory_space=pltpu.VMEM)
SMEM = pl.BlockSpec(memory_space=pltpu.SMEM)


def chunks_of(extent):
    starts = list(range(0, extent, CHUNK))
    return [(start, min(CHUNK, extent - start)) for start in starts]


def three_parts(value):
    high = value.astype(jnp.bfloat16).astype(jnp.float32)
    rest = value - high
    middle = rest.astype(jnp.bfloat16).astype(jnp.float32)
    return high, middle, rest - middle


def with_self(block, tokens, start):
    rows, columns = block.shape
    if rows % 16 == 0:
        place = lax.broadcasted_iota(jnp.int16, (rows, columns), 0) + jnp.int16(start)
        wanted = jnp.broadcast_to(tokens[None], (rows // 16, 16, columns)).reshape(rows, columns)
    else:
        place = lax.broadcasted_iota(jnp.int16, (rows, columns), 0) + jnp.int16(start)
        whole = -(-rows // 16)
        wanted = jnp.broadcast_to(tokens[None], (whole, 16, columns)).reshape(whole * 16, columns)[:rows]
    return jnp.where(place == wanted, block + jnp.bfloat16(1), block)


def put_masses(core, logits_ref, anchors_of, mine_ref, other_ref, mass_ref):
    extent, rows = logits_ref.shape
    top = jnp.max(logits_ref[...], axis=0, keepdims=True)
    total = jnp.zeros((1, rows), jnp.float32)
    for start, size in chunks_of(extent):
        weights = jnp.exp(logits_ref[pl.ds(start, size), :] - top)
        total = total + jnp.sum(weights, axis=0, keepdims=True)
        turned = weights.T.astype(jnp.bfloat16)
        part = jnp.dot(turned, anchors_of(start, size), preferred_element_type=jnp.float32)
        if start == 0:
            mass_ref[...] = part
        else:
            mass_ref[...] += part
    groups, eight, width = mine_ref.shape
    half = width - LANES
    parts = three_parts(top) + three_parts(total)
    stats = jnp.concatenate(list(parts) + [jnp.zeros((LANES - len(parts), rows), jnp.float32)], axis=0)
    stats = stats.T.reshape(groups, eight, LANES).astype(jnp.bfloat16)
    for out_ref, which in ((mine_ref, core), (other_ref, 1 - core)):
        columns = pl.ds(pl.multiple_of(which * half, half), half)
        out_ref[:, :, :half] = mass_ref[:, columns].reshape(groups, eight, half).astype(jnp.bfloat16)
        out_ref[:, :, half:] = stats


def put_other(core, logits_ref, held_ref, other_ref, weights_ref, mass_ref):
    extent, rows = logits_ref.shape
    groups, eight, width = other_ref.shape
    half = width - LANES
    columns = pl.ds(pl.multiple_of((1 - core) * half, half), half)
    top = jnp.max(logits_ref[...], axis=0, keepdims=True)
    total = jnp.zeros((1, rows), jnp.float32)
    for start, size in chunks_of(extent):
        weights = jnp.exp(logits_ref[pl.ds(start, size), :] - top)
        total = total + jnp.sum(weights, axis=0, keepdims=True)
        turned = weights.T.astype(jnp.bfloat16)
        weights_ref[:, start : start + size] = turned
        part = jnp.dot(turned, held_ref[pl.ds(start, size), columns], preferred_element_type=jnp.float32)
        if start == 0:
            mass_ref[...] = part
        else:
            mass_ref[...] += part
    parts = three_parts(top) + three_parts(total)
    stats = jnp.concatenate(list(parts) + [jnp.zeros((LANES - len(parts), rows), jnp.float32)], axis=0)
    other_ref[:, :, :half] = mass_ref[...].reshape(groups, eight, half).astype(jnp.bfloat16)
    other_ref[:, :, half:] = stats.T.reshape(groups, eight, LANES).astype(jnp.bfloat16)


def mine_kernel(place_ref, weights_ref, held_ref, other_ref, turned_ref, mine_ref, mass_ref):
    groups, eight, width = mine_ref.shape
    half = width - LANES
    columns = pl.ds(pl.multiple_of(place_ref[1] * half, half), half)
    for start, size in chunks_of(held_ref.shape[0]):
        block = held_ref[pl.ds(start, size), columns]
        part = jnp.dot(weights_ref[:, start : start + size], block, preferred_element_type=jnp.float32)
        if start == 0:
            mass_ref[...] = part
        else:
            mass_ref[...] += part
    mine_ref[:, :, :half] = mass_ref[...].reshape(groups, eight, half).astype(jnp.bfloat16)
    mine_ref[:, :, half:] = other_ref[:, :, half:]


def first_kernel(place_ref, tokens_ref, anchors_ref, logits_ref, held_ref, turned_ref, mine_ref, other_ref, mass_ref, sems):
    extent = logits_ref.shape[0]
    loads = []
    for i, (start, size) in enumerate(chunks_of(extent)):
        where = pl.ds(start, size)
        loads.append(pltpu.make_async_copy(anchors_ref.at[where], held_ref.at[where], sems.at[i]))
    for load in loads[:AHEAD]:
        load.start()
    shifted = tokens_ref[...] - place_ref[0]
    shifted = jnp.where((shifted >= 0) & (shifted < extent), shifted, -1)
    tokens = jnp.broadcast_to(shifted, (16, shifted.shape[1])).astype(jnp.int16)

    def anchors_of(start, size):
        i = start // CHUNK
        where = pl.ds(start, size)
        loads[i].wait()
        if i + AHEAD < len(loads):
            loads[i + AHEAD].start()
        block = with_self(held_ref[where, :], tokens, start)
        held_ref[where, :] = block
        turned_ref[:, start : start + size] = block.T
        return held_ref[where, :]

    put_masses(place_ref[1], logits_ref, anchors_of, mine_ref, other_ref, mass_ref)


def lane_sum(stats, which):
    lane = lax.broadcasted_iota(jnp.int32, stats.shape, stats.ndim - 1)
    chosen = (lane >= 3 * which) & (lane < 3 * which + 3)
    return jnp.sum(jnp.where(chosen, stats, 0.0), axis=-1, keepdims=True)


def lane_tile(shape, values):
    lane = lax.broadcasted_iota(jnp.int32, shape, len(shape) - 1)
    tile = jnp.zeros(shape, jnp.float32)
    for i, part in enumerate(part for value in values for part in three_parts(value)):
        tile = jnp.where(lane == i, part, tile)
    return tile.astype(jnp.bfloat16)


def pair_kernel(mine_ref, other_ref, *rest):
    out_ref = rest[-1]
    groups, eight, width = mine_ref.shape
    half = width - LANES
    if len(rest) > 1:
        target = sum(ref[...].astype(jnp.float32) for ref in rest[:-1])
        out_ref[:, :, width:] = target.reshape(groups, eight, half).astype(jnp.bfloat16)
    stats = [ref[:, :, half:].astype(jnp.float32) for ref in (mine_ref, other_ref)]
    tops = [lane_sum(stat, 0) for stat in stats]
    top = jnp.maximum(*tops)
    factors = [jnp.exp(each - top) for each in tops]
    total = sum(lane_sum(stat, 1) * factor for stat, factor in zip(stats, factors))
    mine = mine_ref[:, :, :half].astype(jnp.float32) * factors[0]
    other = other_ref[:, :, :half].astype(jnp.float32) * factors[1]
    out_ref[:, :, :half] = (mine + other).astype(jnp.bfloat16)
    out_ref[:, :, half:width] = lane_tile(stats[0].shape, (top, total))


def owner_kernel(full_vocab, first, in_ref, *rest):
    if first:
        out_ref, sum_ref = rest
    else:
        target_ref, out_ref = rest
    width = out_ref.shape[2]
    half = width - LANES
    if first:
        target = jnp.sum(in_ref[:, :, width:].astype(jnp.float32), axis=0)
        sum_ref[...] = target
    else:
        target = target_ref[...]
    stats = in_ref[:, :, half:width].astype(jnp.float32)
    top = lane_sum(stats, 0)
    row_max = jnp.max(top, axis=0, keepdims=True)
    factor = jnp.exp(top - row_max)
    total = jnp.sum(lane_sum(stats, 1) * factor, axis=0)
    mass = jnp.sum(in_ref[:, :, :half].astype(jnp.float32) * factor, axis=0)
    gap = full_vocab * mass / total - target
    sent = gap.astype(jnp.bfloat16)
    squares = jnp.sum(gap * gap, axis=1, keepdims=True)
    inner = jnp.sum(sent.astype(jnp.float32) * mass, axis=1, keepdims=True)
    tile = lane_tile((in_ref.shape[1], LANES), (row_max[0], total, squares, inner))
    out_ref[:, :, :half] = jnp.broadcast_to(sent[None], (in_ref.shape[0],) + sent.shape)
    out_ref[:, :, half:] = jnp.broadcast_to(tile[None], (in_ref.shape[0],) + tile.shape)


def step_kernel(last, place_ref, mine_gap_ref, other_gap_ref, active_ref, base_ref, update_ref, turned_ref, *rest):
    if last:
        out_ref, new_ref, gap_all, sems = rest
    else:
        held_ref, new_ref, weights_ref, other_ref, gap_all, logits_ref, mass_ref = rest
    extent, rows = base_ref.shape
    half = mine_gap_ref.shape[2] - LANES
    core = place_ref[1]
    stats = []
    for gap_ref, which in ((mine_gap_ref, core), (other_gap_ref, 1 - core)):
        columns = pl.ds(pl.multiple_of(which * half, half), half)
        piece = gap_ref[:, :, :half].astype(jnp.float32).reshape(rows, half)
        gap_all[:, columns] = piece.astype(jnp.bfloat16)
        stats.append(gap_ref[:, :, half:].astype(jnp.float32).reshape(rows, LANES).T)

    def joined(which, h):
        return jnp.sum(stats[h][3 * which : 3 * which + 3], axis=0, keepdims=True)

    row_max, total = joined(0, 0), joined(1, 0)
    squares = joined(2, 0) + joined(2, 1)
    inner = joined(3, 0) + joined(3, 1)
    scale = lax.rsqrt(squares / (2 * half) + epsilon)
    slope = scale * inner / total
    active = active_ref[...].astype(jnp.float32)
    copies = []
    for start, size in chunks_of(extent):
        where = pl.ds(start, size)
        turned = jnp.dot(gap_all[...], turned_ref[:, start : start + size], preferred_element_type=jnp.float32)
        back = turned.T * scale
        logits = base_ref[where, :]
        if update_ref is not None:
            logits = logits + update_ref[where, :]
        weights = jnp.exp(logits - row_max)
        change = -step_size * active * weights * (back - slope)
        new_ref[where, :] = change if update_ref is None else update_ref[where, :] + change
        if last:
            copy = pltpu.make_async_copy(new_ref.at[where], out_ref.at[where], sems.at[len(copies)])
            copy.start()
            copies.append(copy)
        else:
            logits_ref[where, :] = logits + change
    for copy in copies:
        copy.wait()
    if not last:
        put_other(core, logits_ref, held_ref, other_ref, weights_ref, mass_ref)


def no_update(kernel):
    def run(place_ref, mine_gap_ref, other_gap_ref, active_ref, base_ref, turned_ref, *rest):
        kernel(place_ref, mine_gap_ref, other_gap_ref, active_ref, base_ref, None, turned_ref, *rest)

    return run


def target_kernel(place_ref, *rest):
    *rest, total_ref, sems = rest
    sources, outs, (tokens_ref, *buffers) = rest[:5], rest[5:-5], rest[-5:]
    copies = [
        pltpu.make_async_copy(source, buffer, sems.at[i])
        for i, (source, buffer) in enumerate(zip(sources, (tokens_ref, *buffers)))
    ]
    for copy in copies:
        copy.start()
    rows, half = outs[0].shape
    columns = pl.ds(pl.multiple_of(place_ref[0] * half, half), half)
    copies[0].wait()
    tokens = tokens_ref[:, columns]
    total = None
    for i in range(2):
        for copy in copies[1 + 2 * i : 3 + 2 * i]:
            copy.wait()
        delta_ref, anchors_ref = buffers[2 * i : 2 * i + 2]
        block = anchors_ref[:, columns].astype(jnp.float32)
        place = lax.broadcasted_iota(jnp.int32, block.shape, 0) + place_ref[1 + i]
        block = jnp.where(place == tokens, block + 1.0, block).astype(jnp.bfloat16)
        part = jnp.dot(delta_ref[...], block, preferred_element_type=jnp.float32)
        total = part if total is None else total + part
    total_ref[...] = total
    for far, out_ref in enumerate(outs):
        group = lax.rem(place_ref[3] + far, len(outs))
        out_ref[...] = total_ref[pl.ds(pl.multiple_of(group * rows, rows), rows), :].astype(jnp.bfloat16)


def shards(expert_delta, small_anchors, small_tokens, base_logits, base_anchors, base_tokens, active_rows):
    f32, bf16 = jnp.float32, jnp.bfloat16
    vocab_count = lax.axis_size(VOCAB)
    vocab_place = lax.axis_index(VOCAB)
    place = lax.axis_index("rows") * vocab_count + vocab_place
    all_rows, small_width = expert_delta.shape
    base_width, anchors = base_anchors.shape
    rows = base_logits.shape[0]
    half = anchors // 2
    width = half + LANES
    eight = 2 * rows // vocab_count
    groups = vocab_count // 2
    pieces = len(chunks_of(base_width))

    core = lax.axis_index("core")
    small_place = jnp.stack([core, place * small_width, (place + 1 - 2 * core) * small_width, lax.axis_index("rows")])
    base_place = jnp.stack([vocab_place * base_width, core])
    small_tokens, base_tokens = small_tokens[None, :], base_tokens[None, :]
    active = active_rows[None, :]
    base = base_logits.T

    swap = [(0, 1), (1, 0)]
    other_delta = lax.ppermute(expert_delta, "core", swap)
    other_anchors = lax.ppermute(small_anchors, "core", swap)
    row_groups = lax.axis_size("rows")
    targets = pl.pallas_call(
        target_kernel,
        out_shape=(jax.ShapeDtypeStruct((rows, half), bf16),) * row_groups,
        in_specs=[SMEM] + [HBM] * 5,
        out_specs=(VMEM,) * row_groups,
        scratch_shapes=[pltpu.VMEM(small_tokens.shape, jnp.int32)]
        + [pltpu.VMEM(each.shape, bf16) for each in (expert_delta, small_anchors)] * 2
        + [pltpu.VMEM((all_rows, half), f32), pltpu.SemaphoreType.DMA((5,))],
        compiler_params=grant(14),
        name="target_parts",
    )(
        small_place,
        *(pltpu.with_memory_space_constraint(each, pltpu.HBM) for each in (small_tokens, expert_delta, small_anchors)),
        other_delta,
        other_anchors,
    )
    base_place, base_tokens, targets = lax.optimization_barrier((base_place, base_tokens, list(targets)))
    for far in range(1, row_groups):
        ring = [(i, (i + far) % row_groups) for i in range(row_groups)]
        targets[far] = lax.ppermute(targets[far], "rows", ring)

    sent_shape = jax.ShapeDtypeStruct((groups, eight, width), bf16)
    held_shape = pltpu.VMEM((base_width, anchors), bf16)
    turned_shape = pltpu.VMEM((anchors, -(-base_width // LANES) * LANES), bf16)
    weights_shape = jax.ShapeDtypeStruct((rows, -(-base_width // LANES) * LANES), bf16)
    update_shape = jax.ShapeDtypeStruct((base_width, rows), f32)
    held, turned, mine, other = pl.pallas_call(
        first_kernel,
        out_shape=(held_shape, turned_shape, sent_shape, sent_shape),
        in_specs=[SMEM, VMEM, HBM, VMEM],
        out_specs=(VMEM,) * 4,
        scratch_shapes=[
            pltpu.VMEM((rows, anchors), f32),
            pltpu.SemaphoreType.DMA((pieces,)),
        ],
        compiler_params=grant(4),
        cost_estimate=pl.CostEstimate(flops=8_000_000_000, bytes_accessed=40_000_000, transcendentals=base_width * rows),
        name="first_masses",
    )(base_place, base_tokens, pltpu.with_memory_space_constraint(base_anchors, pltpu.HBM), base)

    def both(mine, other, *more):
        other = lax.ppermute(other, "core", swap)
        return pl.pallas_call(
            pair_kernel,
            out_shape=jax.ShapeDtypeStruct((groups, eight, width + (half if more else 0)), bf16),
            in_specs=[VMEM] * (2 + len(more)),
            out_specs=VMEM,
            compiler_params=grant(2),
            name="pair",
        )(mine, other, *more)

    sent = both(mine, other, *targets)
    update = None
    for turn in range(ITERATIONS):
        last = turn == ITERATIONS - 1
        got = lax.all_to_all(sent, CHIPS[1:], 0, 0, tiled=True)
        target_shape = jax.ShapeDtypeStruct((eight, half), f32)
        first = turn == 0
        result = pl.pallas_call(
            functools.partial(owner_kernel, float(base_width * vocab_count), first),
            out_shape=(sent_shape, target_shape) if first else sent_shape,
            in_specs=[VMEM] if first else [VMEM, VMEM],
            out_specs=(VMEM, VMEM) if first else VMEM,
            compiler_params=grant(2),
            name="owner",
        )(*((got,) if first else (got, target)))
        if first:
            copies, target = result
        else:
            copies = result
        gaps = lax.all_to_all(copies, CHIPS[1:], 0, 0, tiled=True)
        other_gaps = lax.ppermute(gaps, "core", swap)
        kernel = functools.partial(step_kernel, last)
        operands = [base_place, gaps, other_gaps, active, base] + ([] if update is None else [update]) + [turned] + ([] if last else [held])
        result = pl.pallas_call(
            no_update(kernel) if update is None else kernel,
            out_shape=update_shape if last else (update_shape, weights_shape, sent_shape),
            in_specs=[SMEM] + [VMEM] * (len(operands) - 1),
            out_specs=HBM if last else (VMEM, VMEM, VMEM),
            scratch_shapes=([pltpu.VMEM((base_width, rows), f32)] if last else [])
            + [pltpu.VMEM((rows, anchors), bf16)]
            + (
                [pltpu.SemaphoreType.DMA((pieces,))]
                if last
                else [pltpu.VMEM((base_width, rows), f32), pltpu.VMEM((rows, half), f32)]
            ),
            compiler_params=grant(5),
            name="step",
        )(*operands)
        if last:
            update = result
        else:
            update, weights, other = result
            mine = pl.pallas_call(
                mine_kernel,
                out_shape=sent_shape,
                in_specs=[SMEM, VMEM, VMEM, VMEM, HBM],
                out_specs=VMEM,
                scratch_shapes=[pltpu.VMEM((rows, half), f32)],
                compiler_params=grant(2),
                name="own_half",
            )(base_place, weights, held, other, turned)
            sent = both(mine, other)
    return update.T


def solution(mesh):
    split = Mesh(mesh.devices.reshape(mesh.shape["rows"], 4, 4, 2), ("rows",) + VOCAB)
    everywhere = ("rows",) + VOCAB
    in_specs = (
        P(None, everywhere),
        P(everywhere, None),
        P(),
        P("rows", VOCAB),
        P(VOCAB, None),
        P(),
        P("rows"),
    )

    return jax.shard_map(shards, mesh=split, in_specs=in_specs, out_specs=P("rows", VOCAB), check_vma=False)
```

```python
import functools
import jax
import jax.numpy as jnp
from jax import lax
from jax.experimental import pallas as pl
from jax.experimental.pallas import tpu as pltpu
from jax.sharding import Mesh
from jax.sharding import PartitionSpec as P

ITERATIONS = 3
VOCAB = ("x", "y", "core")
CHIPS = ("rows", "x", "y")
LANES = 128
CHUNK = 512
AHEAD = 3
epsilon = 1e-06
step_size = 2.0


def grant(mebibytes):
    return pltpu.CompilerParams(vmem_limit_bytes=mebibytes * 1024 * 1024)


HBM = pl.BlockSpec(memory_space=pl.ANY)
VMEM = pl.BlockSpec(memory_space=pltpu.VMEM)
SMEM = pl.BlockSpec(memory_space=pltpu.SMEM)


def chunks_of(extent):
    starts = list(range(0, extent, CHUNK))
    return [(start, min(CHUNK, extent - start)) for start in starts]


def three_parts(value):
    high = value.astype(jnp.bfloat16).astype(jnp.float32)
    rest = value - high
    middle = rest.astype(jnp.bfloat16).astype(jnp.float32)
    return high, middle, rest - middle


def with_self(block, tokens, start):
    rows, columns = block.shape
    if rows % 16 == 0:
        place = lax.broadcasted_iota(jnp.int16, (rows, columns), 0) + jnp.int16(start)
        wanted = jnp.broadcast_to(tokens[None], (rows // 16, 16, columns)).reshape(rows, columns)
    else:
        place = lax.broadcasted_iota(jnp.int16, (rows, columns), 0) + jnp.int16(start)
        whole = -(-rows // 16)
        wanted = jnp.broadcast_to(tokens[None], (whole, 16, columns)).reshape(whole * 16, columns)[:rows]
    return jnp.where(place == wanted, block + jnp.bfloat16(1), block)


def put_masses(core, logits_ref, anchors_of, mine_ref, other_ref, mass_ref):
    extent, rows = logits_ref.shape
    top = jnp.max(logits_ref[...], axis=0, keepdims=True)
    total = jnp.zeros((1, rows), jnp.float32)
    for start, size in chunks_of(extent):
        weights = jnp.exp(logits_ref[pl.ds(start, size), :] - top)
        total = total + jnp.sum(weights, axis=0, keepdims=True)
        turned = weights.T.astype(jnp.bfloat16)
        part = jnp.dot(turned, anchors_of(start, size), preferred_element_type=jnp.float32)
        if start == 0:
            mass_ref[...] = part
        else:
            mass_ref[...] += part
    groups, eight, width = mine_ref.shape
    half = width - LANES
    parts = three_parts(top) + three_parts(total)
    stats = jnp.concatenate(list(parts) + [jnp.zeros((LANES - len(parts), rows), jnp.float32)], axis=0)
    stats = stats.T.reshape(groups, eight, LANES).astype(jnp.bfloat16)
    for out_ref, which in ((mine_ref, core), (other_ref, 1 - core)):
        columns = pl.ds(pl.multiple_of(which * half, half), half)
        out_ref[:, :, :half] = mass_ref[:, columns].reshape(groups, eight, half).astype(jnp.bfloat16)
        out_ref[:, :, half:] = stats


def put_other(core, logits_ref, held_ref, other_ref, weights_ref, mass_ref):
    extent, rows = logits_ref.shape
    groups, eight, width = other_ref.shape
    half = width - LANES
    columns = pl.ds(pl.multiple_of((1 - core) * half, half), half)
    top = jnp.max(logits_ref[...], axis=0, keepdims=True)
    total = jnp.zeros((1, rows), jnp.float32)
    for start, size in chunks_of(extent):
        weights = jnp.exp(logits_ref[pl.ds(start, size), :] - top)
        total = total + jnp.sum(weights, axis=0, keepdims=True)
        turned = weights.T.astype(jnp.bfloat16)
        weights_ref[:, start : start + size] = turned
        part = jnp.dot(turned, held_ref[pl.ds(start, size), columns], preferred_element_type=jnp.float32)
        if start == 0:
            mass_ref[...] = part
        else:
            mass_ref[...] += part
    parts = three_parts(top) + three_parts(total)
    stats = jnp.concatenate(list(parts) + [jnp.zeros((LANES - len(parts), rows), jnp.float32)], axis=0)
    other_ref[:, :, :half] = mass_ref[...].reshape(groups, eight, half).astype(jnp.bfloat16)
    other_ref[:, :, half:] = stats.T.reshape(groups, eight, LANES).astype(jnp.bfloat16)


def mine_kernel(place_ref, weights_ref, held_ref, other_ref, turned_ref, mine_ref, mass_ref):
    groups, eight, width = mine_ref.shape
    half = width - LANES
    columns = pl.ds(pl.multiple_of(place_ref[1] * half, half), half)
    for start, size in chunks_of(held_ref.shape[0]):
        block = held_ref[pl.ds(start, size), columns]
        part = jnp.dot(weights_ref[:, start : start + size], block, preferred_element_type=jnp.float32)
        if start == 0:
            mass_ref[...] = part
        else:
            mass_ref[...] += part
    mine_ref[:, :, :half] = mass_ref[...].reshape(groups, eight, half).astype(jnp.bfloat16)
    mine_ref[:, :, half:] = other_ref[:, :, half:]


def first_kernel(place_ref, tokens_ref, anchors_ref, logits_ref, held_ref, turned_ref, mine_ref, other_ref, mass_ref, sems):
    extent = logits_ref.shape[0]
    loads = []
    for i, (start, size) in enumerate(chunks_of(extent)):
        where = pl.ds(start, size)
        loads.append(pltpu.make_async_copy(anchors_ref.at[where], held_ref.at[where], sems.at[i]))
    for load in loads[:AHEAD]:
        load.start()
    shifted = tokens_ref[...] - place_ref[0]
    shifted = jnp.where((shifted >= 0) & (shifted < extent), shifted, -1)
    tokens = jnp.broadcast_to(shifted, (16, shifted.shape[1])).astype(jnp.int16)

    def anchors_of(start, size):
        i = start // CHUNK
        where = pl.ds(start, size)
        loads[i].wait()
        if i + AHEAD < len(loads):
            loads[i + AHEAD].start()
        block = with_self(held_ref[where, :], tokens, start)
        held_ref[where, :] = block
        turned_ref[:, start : start + size] = block.T
        return held_ref[where, :]

    put_masses(place_ref[1], logits_ref, anchors_of, mine_ref, other_ref, mass_ref)


def lane_sum(stats, which):
    lane = lax.broadcasted_iota(jnp.int32, stats.shape, stats.ndim - 1)
    chosen = (lane >= 3 * which) & (lane < 3 * which + 3)
    return jnp.sum(jnp.where(chosen, stats, 0.0), axis=-1, keepdims=True)


def lane_tile(shape, values):
    lane = lax.broadcasted_iota(jnp.int32, shape, len(shape) - 1)
    tile = jnp.zeros(shape, jnp.float32)
    for i, part in enumerate(part for value in values for part in three_parts(value)):
        tile = jnp.where(lane == i, part, tile)
    return tile.astype(jnp.bfloat16)


def pair_kernel(mine_ref, other_ref, *rest):
    out_ref = rest[-1]
    groups, eight, width = mine_ref.shape
    half = width - LANES
    if len(rest) > 1:
        target = sum(ref[...].astype(jnp.float32) for ref in rest[:-1])
        out_ref[:, :, width:] = target.reshape(groups, eight, half).astype(jnp.bfloat16)
    stats = [ref[:, :, half:].astype(jnp.float32) for ref in (mine_ref, other_ref)]
    tops = [lane_sum(stat, 0) for stat in stats]
    top = jnp.maximum(*tops)
    factors = [jnp.exp(each - top) for each in tops]
    total = sum(lane_sum(stat, 1) * factor for stat, factor in zip(stats, factors))
    mine = mine_ref[:, :, :half].astype(jnp.float32) * factors[0]
    other = other_ref[:, :, :half].astype(jnp.float32) * factors[1]
    out_ref[:, :, :half] = (mine + other).astype(jnp.bfloat16)
    out_ref[:, :, half:width] = lane_tile(stats[0].shape, (top, total))


def owner_kernel(full_vocab, first, in_ref, *rest):
    if first:
        out_ref, sum_ref = rest
    else:
        target_ref, out_ref = rest
    width = out_ref.shape[2]
    half = width - LANES
    if first:
        target = jnp.sum(in_ref[:, :, width:].astype(jnp.float32), axis=0)
        sum_ref[...] = target
    else:
        target = target_ref[...]
    stats = in_ref[:, :, half:width].astype(jnp.float32)
    top = lane_sum(stats, 0)
    row_max = jnp.max(top, axis=0, keepdims=True)
    factor = jnp.exp(top - row_max)
    total = jnp.sum(lane_sum(stats, 1) * factor, axis=0)
    mass = jnp.sum(in_ref[:, :, :half].astype(jnp.float32) * factor, axis=0)
    gap = full_vocab * mass / total - target
    sent = gap.astype(jnp.bfloat16)
    squares = jnp.sum(gap * gap, axis=1, keepdims=True)
    inner = jnp.sum(sent.astype(jnp.float32) * mass, axis=1, keepdims=True)
    tile = lane_tile((in_ref.shape[1], LANES), (row_max[0], total, squares, inner))
    out_ref[:, :, :half] = jnp.broadcast_to(sent[None], (in_ref.shape[0],) + sent.shape)
    out_ref[:, :, half:] = jnp.broadcast_to(tile[None], (in_ref.shape[0],) + tile.shape)


def near_kernel(place_ref, gap_ref, turned_ref, *rest):
    part_ref = rest[-1]
    rows = part_ref.shape[0]
    half = gap_ref.shape[2] - LANES
    piece = gap_ref[:, :, :half].astype(jnp.float32).reshape(rows, half).astype(jnp.bfloat16)
    depth = pl.ds(pl.multiple_of(place_ref[1] * half, half), half)
    for start in range(0, turned_ref.shape[1], CHUNK):
        where = pl.ds(start, CHUNK)
        part_ref[:, where] = jnp.dot(piece, turned_ref[depth, where], preferred_element_type=jnp.float32)


def step_kernel(last, place_ref, mine_gap_ref, other_gap_ref, part_ref, active_ref, base_ref, update_ref, turned_ref, *rest):
    if last:
        out_ref, new_ref, sems = rest
    else:
        held_ref, new_ref, weights_ref, other_ref, logits_ref, mass_ref = rest
    extent, rows = base_ref.shape
    half = mine_gap_ref.shape[2] - LANES
    core = place_ref[1]
    stats = [ref[:, :, half:].astype(jnp.float32).reshape(rows, LANES).T for ref in (mine_gap_ref, other_gap_ref)]
    piece = other_gap_ref[:, :, :half].astype(jnp.float32).reshape(rows, half).astype(jnp.bfloat16)
    depth = pl.ds(pl.multiple_of((1 - core) * half, half), half)
    if part_ref is None:
        own_piece = mine_gap_ref[:, :, :half].astype(jnp.float32).reshape(rows, half).astype(jnp.bfloat16)
        own_depth = pl.ds(pl.multiple_of(core * half, half), half)

    def joined(which, h):
        return jnp.sum(stats[h][3 * which : 3 * which + 3], axis=0, keepdims=True)

    row_max, total = joined(0, 0), joined(1, 0)
    squares = joined(2, 0) + joined(2, 1)
    inner = joined(3, 0) + joined(3, 1)
    scale = lax.rsqrt(squares / (2 * half) + epsilon)
    slope = scale * inner / total
    active = active_ref[...].astype(jnp.float32)
    copies = []
    for start, size in chunks_of(extent):
        where = pl.ds(start, size)
        part = jnp.dot(piece, turned_ref[depth, start : start + size], preferred_element_type=jnp.float32)
        if part_ref is None:
            near = jnp.dot(own_piece, turned_ref[own_depth, start : start + size], preferred_element_type=jnp.float32)
        else:
            near = part_ref[:, start : start + size]
        back = (near + part).T * scale
        logits = base_ref[where, :]
        if update_ref is not None:
            logits = logits + update_ref[where, :]
        weights = jnp.exp(logits - row_max)
        change = -step_size * active * weights * (back - slope)
        new_ref[where, :] = change if update_ref is None else update_ref[where, :] + change
        if last:
            copy = pltpu.make_async_copy(new_ref.at[where], out_ref.at[where], sems.at[len(copies)])
            copy.start()
            copies.append(copy)
        else:
            logits_ref[where, :] = logits + change
    for copy in copies:
        copy.wait()
    if not last:
        put_other(core, logits_ref, held_ref, other_ref, weights_ref, mass_ref)


def no_update(kernel):
    def run(place_ref, mine_gap_ref, other_gap_ref, active_ref, base_ref, turned_ref, *rest):
        kernel(place_ref, mine_gap_ref, other_gap_ref, None, active_ref, base_ref, None, turned_ref, *rest)

    return run


def target_kernel(place_ref, *rest):
    *rest, total_ref, sems = rest
    sources, outs, (tokens_ref, *buffers) = rest[:5], rest[5:-5], rest[-5:]
    copies = [
        pltpu.make_async_copy(source, buffer, sems.at[i])
        for i, (source, buffer) in enumerate(zip(sources, (tokens_ref, *buffers)))
    ]
    for copy in copies:
        copy.start()
    rows, half = outs[0].shape
    columns = pl.ds(pl.multiple_of(place_ref[0] * half, half), half)
    copies[0].wait()
    tokens = tokens_ref[:, columns]
    total = None
    for i in range(2):
        for copy in copies[1 + 2 * i : 3 + 2 * i]:
            copy.wait()
        delta_ref, anchors_ref = buffers[2 * i : 2 * i + 2]
        block = anchors_ref[:, columns].astype(jnp.float32)
        place = lax.broadcasted_iota(jnp.int32, block.shape, 0) + place_ref[1 + i]
        block = jnp.where(place == tokens, block + 1.0, block).astype(jnp.bfloat16)
        part = jnp.dot(delta_ref[...], block, preferred_element_type=jnp.float32)
        total = part if total is None else total + part
    total_ref[...] = total
    for far, out_ref in enumerate(outs):
        group = lax.rem(place_ref[3] + far, len(outs))
        out_ref[...] = total_ref[pl.ds(pl.multiple_of(group * rows, rows), rows), :].astype(jnp.bfloat16)


def shards(expert_delta, small_anchors, small_tokens, base_logits, base_anchors, base_tokens, active_rows):
    f32, bf16 = jnp.float32, jnp.bfloat16
    vocab_count = lax.axis_size(VOCAB)
    vocab_place = lax.axis_index(VOCAB)
    place = lax.axis_index("rows") * vocab_count + vocab_place
    all_rows, small_width = expert_delta.shape
    base_width, anchors = base_anchors.shape
    rows = base_logits.shape[0]
    half = anchors // 2
    width = half + LANES
    eight = 2 * rows // vocab_count
    groups = vocab_count // 2
    pieces = len(chunks_of(base_width))

    core = lax.axis_index("core")
    small_place = jnp.stack([core, place * small_width, (place + 1 - 2 * core) * small_width, lax.axis_index("rows")])
    base_place = jnp.stack([vocab_place * base_width, core])
    small_tokens, base_tokens = small_tokens[None, :], base_tokens[None, :]
    active = active_rows[None, :]
    base = base_logits.T

    swap = [(0, 1), (1, 0)]
    other_delta = lax.ppermute(expert_delta, "core", swap)
    other_anchors = lax.ppermute(small_anchors, "core", swap)
    row_groups = lax.axis_size("rows")
    targets = pl.pallas_call(
        target_kernel,
        out_shape=(jax.ShapeDtypeStruct((rows, half), bf16),) * row_groups,
        in_specs=[SMEM] + [HBM] * 5,
        out_specs=(VMEM,) * row_groups,
        scratch_shapes=[pltpu.VMEM(small_tokens.shape, jnp.int32)]
        + [pltpu.VMEM(each.shape, bf16) for each in (expert_delta, small_anchors)] * 2
        + [pltpu.VMEM((all_rows, half), f32), pltpu.SemaphoreType.DMA((5,))],
        compiler_params=grant(14),
        name="target_parts",
    )(
        small_place,
        *(pltpu.with_memory_space_constraint(each, pltpu.HBM) for each in (small_tokens, expert_delta, small_anchors)),
        other_delta,
        other_anchors,
    )
    base_place, base_tokens, targets = lax.optimization_barrier((base_place, base_tokens, list(targets)))
    for far in range(1, row_groups):
        ring = [(i, (i + far) % row_groups) for i in range(row_groups)]
        targets[far] = lax.ppermute(targets[far], "rows", ring)

    sent_shape = jax.ShapeDtypeStruct((groups, eight, width), bf16)
    held_shape = pltpu.VMEM((base_width, anchors), bf16)
    turned_shape = pltpu.VMEM((anchors, -(-base_width // LANES) * LANES), bf16)
    weights_shape = jax.ShapeDtypeStruct((rows, -(-base_width // LANES) * LANES), bf16)
    part_shape = jax.ShapeDtypeStruct((rows, -(-base_width // LANES) * LANES), f32)
    update_shape = jax.ShapeDtypeStruct((base_width, rows), f32)
    held, turned, mine, other = pl.pallas_call(
        first_kernel,
        out_shape=(held_shape, turned_shape, sent_shape, sent_shape),
        in_specs=[SMEM, VMEM, HBM, VMEM],
        out_specs=(VMEM,) * 4,
        scratch_shapes=[
            pltpu.VMEM((rows, anchors), f32),
            pltpu.SemaphoreType.DMA((pieces,)),
        ],
        compiler_params=grant(4),
        cost_estimate=pl.CostEstimate(flops=8_000_000_000, bytes_accessed=40_000_000, transcendentals=base_width * rows),
        name="first_masses",
    )(base_place, base_tokens, pltpu.with_memory_space_constraint(base_anchors, pltpu.HBM), base)

    def both(mine, other, *more):
        other = lax.ppermute(other, "core", swap)
        return pl.pallas_call(
            pair_kernel,
            out_shape=jax.ShapeDtypeStruct((groups, eight, width + (half if more else 0)), bf16),
            in_specs=[VMEM] * (2 + len(more)),
            out_specs=VMEM,
            compiler_params=grant(2),
            name="pair",
        )(mine, other, *more)

    sent = both(mine, other, *targets)
    update = None
    for turn in range(ITERATIONS):
        last = turn == ITERATIONS - 1
        got = lax.all_to_all(sent, CHIPS[1:], 0, 0, tiled=True)
        target_shape = jax.ShapeDtypeStruct((eight, half), f32)
        first = turn == 0
        result = pl.pallas_call(
            functools.partial(owner_kernel, float(base_width * vocab_count), first),
            out_shape=(sent_shape, target_shape) if first else sent_shape,
            in_specs=[VMEM] if first else [VMEM, VMEM],
            out_specs=(VMEM, VMEM) if first else VMEM,
            compiler_params=grant(2),
            name="owner",
        )(*((got,) if first else (got, target)))
        if first:
            copies, target = result
        else:
            copies = result
        gaps = lax.all_to_all(copies, CHIPS[1:], 0, 0, tiled=True)
        other_gaps = lax.ppermute(gaps, "core", swap)
        if update is None:
            parts = []
        else:
            kept = [base, update] + ([] if last else [held])
            part = pl.pallas_call(
                near_kernel,
                out_shape=part_shape,
                in_specs=[SMEM, VMEM, VMEM] + [HBM] * len(kept),
                out_specs=VMEM,
                compiler_params=grant(3),
                name="near_half",
            )(base_place, gaps, turned, *kept)
            parts = [part]
        kernel = functools.partial(step_kernel, last)
        operands = [base_place, gaps, other_gaps, *parts, active, base] + ([] if update is None else [update]) + [turned] + ([] if last else [held])
        result = pl.pallas_call(
            no_update(kernel) if update is None else kernel,
            out_shape=update_shape if last else (update_shape, weights_shape, sent_shape),
            in_specs=[SMEM] + [VMEM] * (len(operands) - 1),
            out_specs=HBM if last else (VMEM, VMEM, VMEM),
            scratch_shapes=([pltpu.VMEM((base_width, rows), f32)] if last else [])
            + (
                [pltpu.SemaphoreType.DMA((pieces,))]
                if last
                else [pltpu.VMEM((base_width, rows), f32), pltpu.VMEM((rows, half), f32)]
            ),
            compiler_params=grant(5),
            name="step",
        )(*operands)
        if last:
            update = result
        else:
            update, weights, other = result
            mine = pl.pallas_call(
                mine_kernel,
                out_shape=sent_shape,
                in_specs=[SMEM, VMEM, VMEM, VMEM, HBM],
                out_specs=VMEM,
                scratch_shapes=[pltpu.VMEM((rows, half), f32)],
                compiler_params=grant(2),
                name="own_half",
            )(base_place, weights, held, other, turned)
            sent = both(mine, other)
    return update.T


def solution(mesh):
    split = Mesh(mesh.devices.reshape(mesh.shape["rows"], 4, 4, 2), ("rows",) + VOCAB)
    everywhere = ("rows",) + VOCAB
    in_specs = (
        P(None, everywhere),
        P(everywhere, None),
        P(),
        P("rows", VOCAB),
        P(VOCAB, None),
        P(),
        P("rows"),
    )

    return jax.shard_map(shards, mesh=split, in_specs=in_specs, out_specs=P("rows", VOCAB), check_vma=False)
```
